128 devices in a mesh: dp: 2 (over y_lo), expert: 64 (over x, z, y_hi, core).
Axes of the slice: x: 4, y: 4 (y_hi: 2, y_lo: 2; y = y_hi * 2 + y_lo), z: 4, core: 2. Of those that a mesh axis runs over, the one named last changes fastest.
Arguments:
- tokens: bfloat16 [2, 2048, 3584], P(None, ('dp', 'expert')), may hold values from -6 to 6
- out_grad: bfloat16 [2, 2048, 3584], P(None, ('dp', 'expert')), may hold values from -6 to 6
- expert_ids: int32 [2, 2048, 4], P(None, ('dp', 'expert')), may hold values from 0 to 31, all different within a row
- route_probs: float32 [2, 2048, 4], P(None, ('dp', 'expert')), may hold values from 0.1 to 0.6
- copy_marks: int32 [2, 32], replicated, may hold values from 0 to 1, as said below
- w_gate: bfloat16 [3584, 32768], P(None, 'expert'), may hold values from -0.09375 to 0.09375
- w_up: bfloat16 [3584, 32768], P(None, 'expert'), may hold values from -0.09375 to 0.09375
- w_down: bfloat16 [3584, 32768], P(None, 'expert'), may hold values from -0.1875 to 0.1875
Outputs:
- moe_out: bfloat16 [2, 2048, 3584], P(None, ('dp', 'expert'))
- input_grad: bfloat16 [2, 2048, 3584], P(None, ('dp', 'expert'))
- grad_gate: float32 [3584, 32768], P('dp', 'expert')
- grad_up: float32 [3584, 32768], P('dp', 'expert')
- grad_down: float32 [3584, 32768], P('dp', 'expert')
The draws below stay inside these ranges and needn't reach their ends.
Inputs may be any that keep to these rules, and one draw needn't show every extreme that they name: `copy_marks`: each row has exactly 16 ones.
All inputs are finite; a program needn't handle non-finite values.
Results may differ from the reference program's by a relative error of at most 0.0064.
Values may be sent and summed in bfloat16 or wider, within the bound.
No kernel may reach another device: no remote copies, remote signals or barrier semaphores. Data moves between devices by JAX's collectives and lax.ppermute only.
A program may use at most 128 MiB of HBM per device.

```python
import jax
import jax.numpy as jnp
from jax import lax

D = 3584
FF = 1024
SPLIT = 2
TOPK = 4
TOK_DEV = 16
FF_DEV = 512
EXPERTS = 32
HOT = 16
CAP = 2
TOKENS = 2048
N_DP = 2
N_EXPERT = 64


def draw_copy_marks(key, part):
    rows = []
    for micro in range(2):
        order = jax.random.permutation(jax.random.fold_in(key, 11 + micro), EXPERTS)
        rows.append((order < HOT).astype(jnp.int32))
    return jnp.stack(rows)


def level_of(stream_key, extent, split, least, high):
    def one(axis_at, blocks):
        draws = jax.random.uniform(jax.random.fold_in(jax.random.fold_in(stream_key, 6), axis_at), (blocks,), jnp.float32, least / len(split), high / len(split))
        return jnp.repeat(jnp.exp(draws), extent[axis_at] // blocks).reshape((-1,) + (1,) * (len(extent) - axis_at - 1))

    level = one(*split[0])
    for cut in split[1:]:
        level = level * one(*cut)
    return level


def choose_distinct(stream_key, rows, number_of, top, lift):
    sequence = jax.random.permutation(jax.random.fold_in(stream_key, 1), number_of)
    favour = sequence
    for power in range(3):
        favour = favour * favour // number_of
    favour = favour * lift // number_of
    lots = jax.random.randint(jax.random.fold_in(stream_key, 2), (rows, number_of), 0, 4096) + favour
    fixed_rows = jax.random.permutation(jax.random.fold_in(stream_key, 3), rows)[jnp.arange(number_of) % rows]
    lots = jnp.where(jnp.arange(rows)[:, None] == fixed_rows[None, :], 1 << 14, lots)
    merit = lots * number_of + jnp.arange(number_of)
    return lax.top_k(merit.astype(jnp.int32), top)[1].astype(jnp.int32)


def scatter_about(rng, shape, deviation, limit, split=(), kind=jnp.bfloat16):
    level = level_of(rng, shape, split, -0.22, 0.18) if split else 1.0
    entries = jax.random.normal(rng, shape, jnp.float32) * deviation * level
    return jnp.minimum(jnp.maximum(entries, -limit), limit).astype(kind)


def setup_inputs(seed: int = 0) -> dict:
    arg_keys = jax.random.split(jax.random.key(seed), 9)
    tokens = scatter_about(arg_keys[0], (2, TOKENS, D), 1.0, 6.0, ((1, 128),))
    out_grad = scatter_about(arg_keys[1], (2, TOKENS, D), 1.0, 6.0, ((1, 128),))
    expert_ids = choose_distinct(arg_keys[2], 2 * TOKENS, EXPERTS, TOPK, 2048).reshape((2, TOKENS, TOPK))
    route_probs = jnp.clip(0.1 + 0.5 * jax.random.uniform(arg_keys[3], (2, TOKENS, TOPK), jnp.float32) ** level_of(arg_keys[3], (2, TOKENS, TOPK), ((1, 128),), -0.2, 0.2), 0.1, 0.6)
    copy_marks = draw_copy_marks(jax.random.fold_in(arg_keys[8], 71), 0)
    w_gate = scatter_about(arg_keys[5], (D, EXPERTS * FF), D ** -0.5, 0.09375, ((1, 64),))
    w_up = scatter_about(arg_keys[6], (D, EXPERTS * FF), D ** -0.5, 0.09375, ((1, 64),))
    w_down = scatter_about(arg_keys[7], (D, EXPERTS * FF), FF ** -0.5, 0.1875, ((1, 64),))
    return {"tokens": tokens, "out_grad": out_grad, "expert_ids": expert_ids, "route_probs": route_probs, "copy_marks": copy_marks, "w_gate": w_gate, "w_up": w_up, "w_down": w_down}


def expert_rows(rows_in, scaled, gate_w, up_w, down_w):
    contract = (((1,), (1,)), ((), ()))
    rows_first = (((0,), (0,)), ((), ()))
    gate_pre = jnp.dot(rows_in, gate_w, preferred_element_type=jnp.float32)
    up_pre = jnp.dot(rows_in, up_w, preferred_element_type=jnp.float32)
    squash = jax.nn.sigmoid(gate_pre)
    active = gate_pre * squash
    hidden = (active * up_pre).astype(jnp.bfloat16)
    part_out = lax.dot_general(hidden, down_w, contract, preferred_element_type=jnp.float32).astype(jnp.bfloat16)
    down_term = lax.dot_general(scaled, hidden, rows_first, preferred_element_type=jnp.float32)
    hidden_grad = jnp.dot(scaled, down_w, preferred_element_type=jnp.float32)
    gate_grad = (hidden_grad * up_pre * squash * (1.0 + gate_pre * (1.0 - squash))).astype(jnp.bfloat16)
    up_grad = (hidden_grad * active).astype(jnp.bfloat16)
    gate_term = lax.dot_general(rows_in, gate_grad, rows_first, preferred_element_type=jnp.float32)
    up_term = lax.dot_general(rows_in, up_grad, rows_first, preferred_element_type=jnp.float32)
    part_dx = lax.dot_general(gate_grad, gate_w, contract, preferred_element_type=jnp.float32)
    part_dx = (part_dx + lax.dot_general(up_grad, up_w, contract, preferred_element_type=jnp.float32)).astype(jnp.bfloat16)
    return part_out, part_dx, gate_term, up_term, down_term


def slot_tables(expert_ids, copy_marks):
    blocks = N_DP * N_EXPERT
    per_block = TOK_DEV * TOPK
    block_slots = 2 * CAP
    slots = blocks * block_slots
    total = blocks * per_block
    labels = jnp.arange(EXPERTS, dtype=jnp.int32)
    result = []
    for micro in range(2):
        flat = expert_ids[micro].reshape(blocks, per_block)
        onehot = (flat[:, :, None] == labels[None, None, :]).astype(jnp.int32)
        earlier = jnp.cumsum(onehot, axis=1) - onehot
        ranked = jnp.sum(earlier * onehot, axis=2)
        marked = jnp.sum(onehot * copy_marks[micro][None, None, :], axis=2)
        kept = (ranked < CAP) | ((marked > 0) & (ranked < 2 * CAP))
        starts = jnp.arange(blocks, dtype=jnp.int32)[:, None] * block_slots
        column = jnp.where(kept, starts + ranked, slots).reshape(total).astype(jnp.int32)
        owner = flat.reshape(total).astype(jnp.int32)
        table = jnp.full((EXPERTS, slots + 1), total, dtype=jnp.int32)
        table = table.at[owner, column].set(jnp.arange(total, dtype=jnp.int32))
        result.append(table[:, :slots])
    return jnp.stack(result)


def reference(tokens, out_grad, expert_ids, route_probs, copy_marks, w_gate, w_up, w_down):
    tables = slot_tables(expert_ids, copy_marks)
    total = TOKENS * TOPK
    slots = N_DP * N_EXPERT * 2 * CAP
    probs_flat = route_probs.reshape(2, total)

    def per_expert(carry, expert):
        moe_acc, grad_acc = carry
        start = expert * FF
        gate_w = lax.dynamic_slice_in_dim(w_gate, start, FF, 1)
        up_w = lax.dynamic_slice_in_dim(w_up, start, FF, 1)
        down_w = lax.dynamic_slice_in_dim(w_down, start, FF, 1)
        gate_sum = jnp.zeros((D, FF), jnp.float32)
        up_sum = jnp.zeros((D, FF), jnp.float32)
        down_sum = jnp.zeros((D, FF), jnp.float32)
        for micro in range(2):
            rows = tables[micro, expert]
            valid = rows < total
            safe = jnp.where(valid, rows, 0).astype(jnp.int32)
            token = (safe // TOPK).astype(jnp.int32)
            weight = jnp.where(valid, probs_flat[micro][safe], jnp.zeros((), jnp.float32))
            rows_in = jnp.where(valid[:, None], tokens[micro][token], jnp.zeros((), jnp.bfloat16))
            scaled = (weight[:, None] * out_grad[micro][token].astype(jnp.float32)).astype(jnp.bfloat16)
            out_sum = jnp.zeros((slots, D), jnp.float32)
            dx_sum = jnp.zeros((slots, D), jnp.float32)
            gate_parts = []
            up_parts = []
            down_parts = []
            for part in range(SPLIT):
                low = part * FF_DEV
                part_out, part_dx, gate_term, up_term, down_term = expert_rows(
                    rows_in, scaled, gate_w[:, low:low + FF_DEV], up_w[:, low:low + FF_DEV], down_w[:, low:low + FF_DEV])
                out_sum = out_sum + part_out.astype(jnp.float32)
                dx_sum = dx_sum + part_dx.astype(jnp.float32)
                gate_parts.append(gate_term)
                up_parts.append(up_term)
                down_parts.append(down_term)
            gate_sum = gate_sum + jnp.concatenate(gate_parts, axis=1)
            up_sum = up_sum + jnp.concatenate(up_parts, axis=1)
            down_sum = down_sum + jnp.concatenate(down_parts, axis=1)
            moe_acc = moe_acc.at[micro, token].add(weight[:, None] * out_sum)
            grad_acc = grad_acc.at[micro, token].add(jnp.where(valid[:, None], dx_sum, jnp.zeros((), jnp.float32)))
        return (moe_acc, grad_acc), (gate_sum, up_sum, down_sum)

    start_carry = (jnp.zeros((2, TOKENS, D), jnp.float32), jnp.zeros((2, TOKENS, D), jnp.float32))
    (moe_acc, grad_acc), grads = lax.scan(per_expert, start_carry, jnp.arange(EXPERTS, dtype=jnp.int32))

    def arrange(stacked):
        return jnp.moveaxis(stacked, 0, 1).reshape(D, EXPERTS * FF)

    return (moe_acc.astype(jnp.bfloat16), grad_acc.astype(jnp.bfloat16),
            arrange(grads[0]), arrange(grads[1]), arrange(grads[2]))
```

```python
import jax
import jax.numpy as jnp
from jax import lax
from jax.sharding import PartitionSpec as P

SPLIT = 2
AXES = ("dp", "expert")


def near_groups(n_dp, n_ep):
    groups = []
    for side in range(n_dp):
        for core in range(SPLIT):
            groups.append(
                [((e % n_dp) ^ side) * n_ep + SPLIT * e + core for e in range(n_ep // SPLIT)]
            )
    return groups


def exchange(x, groups):
    return lax.all_to_all(
        x, AXES, split_axis=0, concat_axis=0, tiled=True, axis_index_groups=groups
    )


def slot_tables(expert_ids, route_probs, marks, experts, capacity):
    micros, tok_rows, topk = expert_ids.shape
    slots = 2 * capacity
    labels = jnp.arange(experts, dtype=jnp.int32)
    hit = expert_ids[:, :, :, None] == labels
    member = jnp.any(hit, axis=2)
    prob = jnp.sum(jnp.where(hit, route_probs[:, :, :, None], 0.0), axis=2)
    rows = jnp.arange(tok_rows)
    before = (rows[None, :] < rows[:, None])[None, :, :, None] & member[:, None, :, :]
    ranked = jnp.sum(before.astype(jnp.int32), axis=2)
    limit = jnp.where(marks > 0, 2 * capacity, capacity)
    kept = member & (ranked < limit[:, None, :])
    place = jnp.where(kept, ranked, -1)
    place = place.transpose(2, 0, 1)
    prob = prob.transpose(2, 0, 1)
    rank = jnp.arange(slots, dtype=jnp.int32)
    same = jnp.eye(micros, dtype=bool)
    chosen = (place[:, None, None, :, :] == rank[None, None, :, None, None]) & same[
        None, :, None, :, None
    ]
    mixing = jnp.where(chosen, prob[:, None, None, :, :], 0.0)
    places = experts * micros * slots
    return (
        chosen.reshape(places, micros * tok_rows),
        mixing.reshape(places, micros * tok_rows),
    )


CONTRACT = (((1,), (1,)), ((), ()))
ROWS_FIRST = (((0,), (0,)), ((), ()))


def mm(a, b, dims=(((1,), (0,)), ((), ()))):
    return lax.dot_general(a, b, dims, preferred_element_type=jnp.float32)


def local(tokens, out_grad, expert_ids, route_probs, copy_marks, w_gate, w_up, w_down):
    n_dp = lax.axis_size("dp")
    n_ep = lax.axis_size("expert")
    devices = n_dp * n_ep
    experts = n_ep // SPLIT
    micros, tok_rows, width = tokens.shape
    topk = expert_ids.shape[2]
    capacity = max(1, tok_rows * topk // experts)
    group_rows = micros * 2 * capacity
    half_width = width // n_dp
    half = lax.axis_index("dp")
    groups = near_groups(n_dp, n_ep)
    cores = [(i, i ^ 1) for i in range(devices)]
    pairs = [(i, (i + n_ep) % devices) for i in range(devices)]

    def core_swap(x):
        return lax.ppermute(x, AXES, cores)

    def pair_swap(x):
        return lax.ppermute(x, AXES, pairs)

    def mine(x):
        return lax.dynamic_slice_in_dim(x, half * half_width, half_width, 1)

    def theirs(x):
        return lax.dynamic_slice_in_dim(x, (1 - half) * half_width, half_width, 1)

    chosen, mixing = slot_tables(expert_ids, route_probs, copy_marks, experts, capacity)
    picked = chosen.astype(jnp.bfloat16)
    flat_tokens = tokens.reshape(micros * tok_rows, width)
    flat_cot = out_grad.reshape(micros * tok_rows, width)
    moved = mm(picked, flat_tokens).astype(jnp.bfloat16)
    slot_prob = jnp.sum(mixing, axis=1, keepdims=True)
    spread = (slot_prob * mm(picked, flat_cot)).astype(jnp.bfloat16)

    def dispatch(x):
        return exchange(x.reshape(experts, group_rows, width), groups).reshape(-1, width)

    x_own = dispatch(moved)
    c_own = dispatch(spread)
    x_oth = core_swap(x_own)
    xp_own = pair_swap(theirs(x_own))
    xp_oth = core_swap(xp_own)

    def forward(x):
        gate_pre = mm(x, w_gate)
        up_pre = mm(x, w_up)
        squash = jax.nn.sigmoid(gate_pre)
        active = gate_pre * squash
        hidden = (active * up_pre).astype(jnp.bfloat16)
        part_out = mm(hidden, w_down, CONTRACT).astype(jnp.bfloat16)
        return gate_pre, up_pre, squash, active, hidden, part_out

    def backward(c, kept):
        gate_pre, up_pre, squash, active, hidden, _ = kept
        hidden_grad = mm(c, w_down)
        gate_grad = (hidden_grad * up_pre * squash * (1.0 + gate_pre * (1.0 - squash))).astype(
            jnp.bfloat16
        )
        up_grad = (hidden_grad * active).astype(jnp.bfloat16)
        part_dx = (mm(gate_grad, w_gate, CONTRACT) + mm(up_grad, w_up, CONTRACT)).astype(
            jnp.bfloat16
        )
        return gate_grad, up_grad, part_dx

    def send_back(own, oth):
        other = core_swap(oth)
        total = (own.astype(jnp.float32) + other.astype(jnp.float32)).astype(jnp.bfloat16)
        return exchange(total.reshape(experts, group_rows, width), groups).reshape(-1, width)

    own = forward(x_own)
    oth = forward(x_oth)
    back_out = send_back(own[5], oth[5])

    c_oth = core_swap(c_own)
    cp_own = pair_swap(theirs(c_own))
    cp_oth = core_swap(cp_own)
    gg_own, ug_own, dx_own = backward(c_own, own)
    gg_oth, ug_oth, dx_oth = backward(c_oth, oth)
    back_dx = send_back(dx_own, dx_oth)

    def both(a, b):
        return jnp.concatenate([a, b], axis=0)

    x_cols = jnp.concatenate([mine(x_own), mine(x_oth), xp_own, xp_oth], axis=0)
    c_cols = jnp.concatenate([mine(c_own), mine(c_oth), cp_own, cp_oth], axis=0)

    def whole(a, b):
        here = both(a, b)
        return both(here, pair_swap(here))

    hidden = whole(own[4], oth[4])
    gate_grad = whole(gg_own, gg_oth)
    up_grad = whole(ug_own, ug_oth)
    grad_down = mm(c_cols, hidden, ROWS_FIRST)
    grad_gate = mm(x_cols, gate_grad, ROWS_FIRST)
    grad_up = mm(x_cols, up_grad, ROWS_FIRST)

    def piece(x):
        return lax.reduce_precision(x, exponent_bits=8, mantissa_bits=7)

    high = piece(mixing)
    middle = piece(mixing - high)
    low = mixing - high - middle
    split = jnp.concatenate([high, middle, low], axis=1).astype(jnp.bfloat16)
    sums = mm(split, back_out, ROWS_FIRST).reshape(3, micros, tok_rows, width)
    moe = (sums[0] + (sums[1] + sums[2])).astype(jnp.bfloat16)
    grad_in = mm(picked, back_dx, ROWS_FIRST).reshape(micros, tok_rows, width)
    return (moe, grad_in.astype(jnp.bfloat16), grad_gate, grad_up, grad_down)


def solution(mesh):
    tok = P(None, AXES, None)
    return jax.shard_map(
        local,
        mesh=mesh,
        in_specs=(tok, tok, tok, tok, P(), P(None, "expert"), P(None, "expert"), P(None, "expert")),
        out_specs=(tok, tok, P("dp", "expert"), P("dp", "expert"), P("dp", "expert")),
        check_vma=False,
    )
```

```python
import math

import jax
import jax.numpy as jnp
from jax import lax
from jax.experimental import pallas as pl
from jax.experimental.pallas import tpu as pltpu
from jax.sharding import PartitionSpec as P


SPLIT = 2
AXES = ("dp", "expert")
PLAIN = (((1,), (0,)), ((), ()))
CONTRACT = (((1,), (1,)), ((), ()))
ROWS_FIRST = (((0,), (0,)), ((), ()))
VMEM = pl.BlockSpec(memory_space=pltpu.VMEM)
SMEM = pl.BlockSpec(memory_space=pltpu.SMEM)
HBM = pl.BlockSpec(memory_space=pltpu.HBM)


def near_groups(n_dp, n_ep):
    groups = []
    for side in range(n_dp):
        for core in range(SPLIT):
            groups.append(
                [((e % n_dp) ^ side) * n_ep + SPLIT * e + core for e in range(n_ep // SPLIT)]
            )
    return groups


def exchange(x, groups):
    return lax.all_to_all(
        x, AXES, split_axis=0, concat_axis=0, tiled=True, axis_index_groups=groups
    )


def mm(a, b, dims=PLAIN):
    return lax.dot_general(a, b, dims, preferred_element_type=jnp.float32)


def bf(*shape):
    return jax.ShapeDtypeStruct(shape, jnp.bfloat16)


def in_hbm(x):
    return pltpu.with_memory_space_constraint(x, pltpu.HBM)


def call(kernel, outs, ins, flops, in_specs, out_specs=None, scratch=()):
    size = sum(math.prod(x.shape) * x.dtype.itemsize for x in tuple(ins) + tuple(outs))
    return pl.pallas_call(
        kernel,
        out_shape=outs,
        in_specs=in_specs,
        out_specs=out_specs or [VMEM] * len(outs),
        scratch_shapes=list(scratch),
        compiler_params=pltpu.CompilerParams(vmem_limit_bytes=28 << 20),
        cost_estimate=pl.CostEstimate(flops=flops, bytes_accessed=size, transcendentals=0),
    )(*ins)


def pack_body(slots, capacity, ids_ref, prob_ref, marks_ref, tok_ref, cot_ref,
              sent_ref, pick_ref, split_ref, tok_buf, cot_buf, buf, sems):
    micros, topk, per_micro = ids_ref.shape
    experts = marks_ref.shape[1]
    places, rows = pick_ref.shape
    width = tok_ref.shape[1]
    fetch_tok = pltpu.make_async_copy(tok_ref, tok_buf, sems.at[0])
    fetch_cot = pltpu.make_async_copy(cot_ref, cot_buf, sems.at[1])
    fetch_tok.start()
    fetch_cot.start()
    ids = jnp.concatenate([ids_ref[m] for m in range(micros)], axis=1)
    probs = jnp.concatenate([prob_ref[m] for m in range(micros)], axis=1)
    place = lax.broadcasted_iota(jnp.int32, (places, rows), 0)
    token = lax.broadcasted_iota(jnp.int32, (places, rows), 1)
    expert = place // (micros * slots)
    micro = (place // slots) % micros
    hit = jnp.zeros((places, rows), jnp.float32)
    prob = jnp.zeros((places, rows), jnp.float32)
    for k in range(topk):
        same = ids[k : k + 1, :] == expert
        hit = hit + jnp.where(same, 1.0, 0.0)
        prob = prob + jnp.where(same, probs[k : k + 1, :], 0.0)
    down = lax.broadcasted_iota(jnp.int32, (rows, rows), 0)
    across = lax.broadcasted_iota(jnp.int32, (rows, rows), 1)
    earlier = (down < across) & (across // per_micro == down // per_micro)
    earlier = jnp.where(earlier, 1.0, 0.0).astype(jnp.bfloat16)
    ranked = mm(hit.astype(jnp.bfloat16), earlier)
    label = lax.broadcasted_iota(jnp.int32, (places, experts), 1)
    spot = lax.broadcasted_iota(jnp.int32, (places, experts), 0)
    marks = jnp.zeros((places, experts), jnp.float32)
    for m in range(micros):
        mark = jnp.where(marks_ref[m : m + 1, :] > 0, 1.0, 0.0)
        marks = marks + jnp.where((spot // slots) % micros == m, mark, 0.0)
    marks = jnp.where(label == spot // (micros * slots), marks, 0.0)
    limit = capacity * (1.0 + jnp.sum(marks, axis=1, keepdims=True))
    chosen = (hit > 0.5) & (micro == token // per_micro) & (ranked < limit)
    chosen = chosen & (ranked == (place % slots).astype(jnp.float32))
    picked = jnp.where(chosen, 1.0, 0.0).astype(jnp.bfloat16)
    weight = jnp.where(chosen, prob, 0.0)
    slot_prob = jnp.sum(weight, axis=1, keepdims=True)
    high = weight.astype(jnp.bfloat16)
    rest = weight - high.astype(jnp.float32)
    middle = rest.astype(jnp.bfloat16)
    low = (rest - middle.astype(jnp.float32)).astype(jnp.bfloat16)
    pick_ref[...] = picked
    split_ref[0] = high
    split_ref[1] = middle
    split_ref[2] = low
    fetch_tok.wait()
    buf[:, :width] = mm(picked, tok_buf[...]).astype(jnp.bfloat16)
    first = pltpu.make_async_copy(
        buf.at[:, pl.ds(0, width)], sent_ref.at[:, pl.ds(0, width)], sems.at[2]
    )
    first.start()
    fetch_cot.wait()
    buf[:, width:] = (slot_prob * mm(picked, cot_buf[...])).astype(jnp.bfloat16)
    second = pltpu.make_async_copy(
        buf.at[:, pl.ds(width, width)], sent_ref.at[:, pl.ds(width, width)], sems.at[3]
    )
    second.start()
    first.wait()
    second.wait()


def cut_body(start_ref, rows_ref, out_ref, sems):
    take = out_ref.shape[1] // 2
    width = rows_ref.shape[1] // 2
    start = pl.multiple_of(start_ref[0], 128)
    copies = [
        pltpu.make_async_copy(
            rows_ref.at[:, pl.ds(pl.multiple_of(start + i * width, 128), take)],
            out_ref.at[:, pl.ds(i * take, take)],
            sems.at[i],
        )
        for i in range(2)
    ]
    for copy in copies:
        copy.start()
    for copy in copies:
        copy.wait()


def slopes(gate_pre, up_pre, hidden_grad):
    squash = jax.nn.sigmoid(gate_pre)
    active = gate_pre * squash
    hidden = (active * up_pre).astype(jnp.bfloat16)
    slope = squash * (1.0 + gate_pre * (1.0 - squash))
    gate_grad = (hidden_grad * up_pre * slope).astype(jnp.bfloat16)
    up_grad = (hidden_grad * active).astype(jnp.bfloat16)
    return hidden, gate_grad, up_grad


def own_body(pieces, rows_ref, wg_ref, wu_ref, wd_ref, hid_ref, gg_ref, ug_ref,
             wg_out, wu_out, wd_out, xbuf, cbuf, sems):
    width = wg_ref.shape[0]
    size = width // pieces
    fetches = []
    for i in range(pieces):
        low = i * size
        span = pl.ds(low, size)
        moves = (
            (rows_ref.at[:, span], xbuf.at[:, span]),
            (wg_ref.at[span, :], wg_out.at[span, :]),
            (wu_ref.at[span, :], wu_out.at[span, :]),
            (rows_ref.at[:, pl.ds(width + low, size)], cbuf.at[:, span]),
            (wd_ref.at[span, :], wd_out.at[span, :]),
        )
        fetches.append(
            [pltpu.make_async_copy(a, b, sems.at[i, k]) for k, (a, b) in enumerate(moves)]
        )
    for fetch in fetches:
        for copy in fetch:
            copy.start()
    gate_pre = up_pre = hidden_grad = 0.0
    for i in range(pieces):
        low, high = i * size, (i + 1) * size
        for copy in fetches[i]:
            copy.wait()
        x = xbuf[:, low:high]
        gate_pre = gate_pre + mm(x, wg_out[low:high, :])
        up_pre = up_pre + mm(x, wu_out[low:high, :])
        hidden_grad = hidden_grad + mm(cbuf[:, low:high], wd_out[low:high, :])
    values = slopes(gate_pre, up_pre, hidden_grad)
    for ref, value in zip((hid_ref, gg_ref, ug_ref), values):
        ref[...] = value


def oth_body(rows_ref, wg_ref, wu_ref, wd_ref, h_ref, g_ref, u_ref,
             hid_ref, gg_ref, ug_ref, xbuf, cbuf, sems):
    width = wg_ref.shape[0]
    fetch_x = pltpu.make_async_copy(rows_ref.at[:, pl.ds(0, width)], xbuf, sems.at[0])
    fetch_c = pltpu.make_async_copy(rows_ref.at[:, pl.ds(width, width)], cbuf, sems.at[1])
    fetch_x.start()
    fetch_c.start()
    fetch_x.wait()
    x = xbuf[...]
    gate_pre = mm(x, wg_ref[...])
    up_pre = mm(x, wu_ref[...])
    fetch_c.wait()
    hidden_grad = mm(cbuf[...], wd_ref[...])
    values = slopes(gate_pre, up_pre, hidden_grad)
    rows = h_ref.shape[0]
    for ref, prior, value in zip((hid_ref, gg_ref, ug_ref), (h_ref, g_ref, u_ref), values):
        ref[0:rows, :] = prior[...]
        ref[rows : 2 * rows, :] = value


def out_body(hid_ref, wd_ref, out_ref):
    rows = out_ref.shape[0]
    hidden = hid_ref[rows : 2 * rows, :]
    out_ref[...] = mm(hidden, wd_ref[...], CONTRACT).astype(jnp.bfloat16)


def dx_body(gg_ref, ug_ref, wg_ref, wu_ref, dx_ref):
    rows = dx_ref.shape[0]
    dx = mm(gg_ref[rows : 2 * rows, :], wg_ref[...], CONTRACT)
    dx = dx + mm(ug_ref[rows : 2 * rows, :], wu_ref[...], CONTRACT)
    dx_ref[...] = dx.astype(jnp.bfloat16)


def plus(part, other):
    here = part.astype(jnp.bfloat16).astype(jnp.float32)
    return (here + other.astype(jnp.float32)).astype(jnp.bfloat16)


def out_add_body(hid_ref, wd_ref, other_ref, out_ref):
    rows = out_ref.shape[0]
    out_ref[...] = plus(mm(hid_ref[0:rows, :], wd_ref[...], CONTRACT), other_ref[...])


def dx_add_body(pieces, gg_ref, ug_ref, wg_ref, wu_ref, other_ref, left_ref, out_ref, buf, sems):
    rows, width = left_ref.shape
    copies = [
        pltpu.make_async_copy(left_ref, out_ref.at[:, pl.ds(0, width)], sems.at[pieces])
    ]
    copies[0].start()
    gate_grad = gg_ref[0:rows, :]
    up_grad = ug_ref[0:rows, :]
    size = width // pieces
    for i in range(pieces):
        low, high = i * size, (i + 1) * size
        dx = mm(gate_grad, wg_ref[low:high, :], CONTRACT)
        dx = dx + mm(up_grad, wu_ref[low:high, :], CONTRACT)
        buf[:, low:high] = plus(dx, other_ref[:, low:high])
        copy = pltpu.make_async_copy(
            buf.at[:, pl.ds(low, size)], out_ref.at[:, pl.ds(width + low, size)], sems.at[i]
        )
        copy.start()
        copies.append(copy)
    for copy in copies:
        copy.wait()


def turn_body(half_ref, first_ref, second_ref, out_ref):
    rows = first_ref.shape[0]
    out_ref[:, 0:rows] = first_ref[...].T
    out_ref[:, rows : 2 * rows] = second_ref[...].T


def turn(half, first, second, cut):
    rows, wide = first.shape
    block = 256
    tall = wide if cut else wide // 2
    steps = tall // block
    per = steps // 2
    if cut:
        spec = pl.BlockSpec((rows, block), lambda i, h: (0, i))
    else:
        spec = pl.BlockSpec((rows, block), lambda i, h: (0, h[0] * per + i + i // per * per))
    return pl.pallas_call(
        turn_body,
        out_shape=bf(tall, 2 * rows),
        grid_spec=pltpu.PrefetchScalarGridSpec(
            num_scalar_prefetch=1,
            grid=(steps,),
            in_specs=[spec, spec],
            out_specs=pl.BlockSpec((block, 2 * rows), lambda i, h: (i, 0)),
        ),
        compiler_params=pltpu.CompilerParams(vmem_limit_bytes=28 << 20),
    )(half, first, second)


def grad_body(near_ref, far_ref, here_ref, there_ref, out_ref):
    out_ref[...] = mm(near_ref[...], here_ref[...]) + mm(far_ref[...], there_ref[...])


def weight_grad(near, far, here, there, second):
    wide, rows = near.shape
    part = here.shape[1]
    tall = wide // 2
    block = 256
    steps = tall // block
    start = steps if second else 0
    lhs = pl.BlockSpec((block, rows), lambda i: (start + i, 0))
    whole = pl.BlockSpec((rows, part), lambda i: (0, 0))
    return pl.pallas_call(
        grad_body,
        out_shape=jax.ShapeDtypeStruct((tall, part), jnp.float32),
        grid=(steps,),
        in_specs=[lhs, lhs, whole, whole],
        out_specs=pl.BlockSpec((block, part), lambda i: (i, 0)),
        compiler_params=pltpu.CompilerParams(vmem_limit_bytes=28 << 20),
        cost_estimate=pl.CostEstimate(
            flops=4 * rows * tall * part, bytes_accessed=8 << 20, transcendentals=0
        ),
    )(near, far, here, there)


def combine_body(pieces, back_ref, pick_ref, split_ref, moe_ref, dx_ref, buf, sems):
    width = moe_ref.shape[1]
    size = width // pieces
    copies = []
    for i in range(2 * pieces):
        span = pl.ds(i * size, size)
        copies.append(pltpu.make_async_copy(back_ref.at[:, span], buf.at[:, span], sems.at[i]))
    for copy in copies:
        copy.start()
    for i in range(pieces):
        low, high = i * size, (i + 1) * size
        copies[i].wait()
        rows = buf[:, low:high]
        small = mm(split_ref[1], rows, ROWS_FIRST) + mm(split_ref[2], rows, ROWS_FIRST)
        moe = mm(split_ref[0], rows, ROWS_FIRST) + small
        moe_ref[:, low:high] = moe.astype(jnp.bfloat16)
    for i in range(pieces):
        low, high = i * size, (i + 1) * size
        copies[pieces + i].wait()
        dx = mm(pick_ref[...], buf[:, width + low : width + high], ROWS_FIRST)
        dx_ref[:, low:high] = dx.astype(jnp.bfloat16)


def combine(back, picked, split, pieces):
    places, double = back.shape
    width = double // 2
    rows = picked.shape[1]

    def body(*refs):
        combine_body(pieces, *refs)

    return call(
        body,
        (bf(rows, width), bf(rows, width)),
        (in_hbm(back), picked, split),
        8 * rows * places * width,
        [HBM, VMEM, VMEM],
        scratch=(
            pltpu.VMEM((places, double), jnp.bfloat16),
            pltpu.SemaphoreType.DMA((2 * pieces,)),
        ),
    )


def local(tokens, out_grad, expert_ids, route_probs, copy_marks, w_gate, w_up, w_down):
    n_dp = lax.axis_size("dp")
    n_ep = lax.axis_size("expert")
    devices = n_dp * n_ep
    experts = n_ep // SPLIT
    micros, tok_rows, width = tokens.shape
    topk = expert_ids.shape[2]
    capacity = max(1, tok_rows * topk // experts)
    slots = 2 * capacity
    group_rows = micros * slots
    places = experts * group_rows
    half_width = width // n_dp
    part = w_gate.shape[1]
    flat_rows = micros * tok_rows
    half = lax.axis_index("dp").astype(jnp.int32)
    groups = near_groups(n_dp, n_ep)
    cores = [(i, i ^ 1) for i in range(devices)]
    pairs = [(i, (i + n_ep) % devices) for i in range(devices)]
    unit = 2 * places * part * width

    def core_swap(x):
        return lax.ppermute(x, AXES, cores)

    def pair_swap(x):
        return lax.ppermute(x, AXES, pairs)

    def travel(x):
        return exchange(x.reshape(experts, group_rows, 2 * width), groups).reshape(-1, 2 * width)

    def pack(*refs):
        pack_body(slots, capacity, *refs)

    sent, picked, split = call(
        pack,
        (
            pltpu.HBM((places, 2 * width), jnp.bfloat16),
            bf(places, flat_rows),
            bf(3, places, flat_rows),
        ),
        (
            expert_ids.transpose(0, 2, 1),
            route_probs.transpose(0, 2, 1),
            copy_marks,
            in_hbm(tokens.reshape(flat_rows, width)),
            in_hbm(out_grad.reshape(flat_rows, width)),
        ),
        4 * places * flat_rows * width,
        [VMEM] * 3 + [HBM] * 2,
        [HBM, VMEM, VMEM],
        (
            pltpu.VMEM((flat_rows, width), jnp.bfloat16),
            pltpu.VMEM((flat_rows, width), jnp.bfloat16),
            pltpu.VMEM((places, 2 * width), jnp.bfloat16),
            pltpu.SemaphoreType.DMA((4,)),
        ),
    )
    own = travel(sent)
    oth = core_swap(own)
    (theirs,) = call(
        cut_body,
        (bf(places, width),),
        (((1 - half) * half_width).reshape(1), own),
        0,
        [SMEM, HBM],
        [VMEM],
        (pltpu.SemaphoreType.DMA((2,)),),
    )
    pair_own = pair_swap(theirs)

    pieces = 4

    def begin(*refs):
        own_body(pieces, *refs)

    def finish(*refs):
        dx_add_body(pieces, *refs)

    buffers = (
        pltpu.VMEM((places, width), jnp.bfloat16),
        pltpu.VMEM((places, width), jnp.bfloat16),
    )
    mid = bf(places, part)
    mids = bf(2 * places, part)
    *first, wg, wu, wd = call(
        begin,
        (mid,) * 3 + (bf(width, part),) * 3,
        (own, *map(in_hbm, (w_gate, w_up, w_down))),
        3 * unit,
        [HBM] * 4,
        scratch=buffers + (pltpu.SemaphoreType.DMA((pieces, 5)),),
    )
    hid, gg, ug = call(
        oth_body,
        (mids,) * 3,
        (oth, wg, wu, wd, *first),
        3 * unit,
        [HBM] + [VMEM] * 6,
        scratch=buffers + (pltpu.SemaphoreType.DMA((2,)),),
    )
    row = bf(places, width)
    (out_oth,) = call(out_body, (row,), (hid, wd), unit, [VMEM] * 2)
    (dx_oth,) = call(dx_body, (row,), (gg, ug, wg, wu), 2 * unit, [VMEM] * 4)
    out_other = core_swap(out_oth)
    dx_other = core_swap(dx_oth)
    hid_there = pair_swap(hid)
    gg_there = pair_swap(gg)
    ug_there = pair_swap(ug)

    (left,) = call(out_add_body, (row,), (hid, wd, out_other), unit, [VMEM] * 3)
    (total,) = call(
        finish,
        (pltpu.HBM((places, 2 * width), jnp.bfloat16),),
        (gg, ug, wg, wu, dx_other, left),
        2 * unit,
        [VMEM] * 6,
        [HBM],
        (
            pltpu.VMEM((places, width), jnp.bfloat16),
            pltpu.SemaphoreType.DMA((pieces + 1,)),
        ),
    )
    back = travel(total)
    pair_oth = core_swap(pair_own)
    h = half.reshape(1)
    near = turn(h, own, oth, False)
    far = turn(h, pair_own, pair_oth, True)
    grad_down = weight_grad(near, far, hid, hid_there, True)
    grad_gate = weight_grad(near, far, gg, gg_there, False)
    grad_up = weight_grad(near, far, ug, ug_there, False)
    moe, grad_in = combine(back, picked, split, pieces)
    return (
        moe.reshape(micros, tok_rows, width),
        grad_in.reshape(micros, tok_rows, width),
        grad_gate,
        grad_up,
        grad_down,
    )


def solution(mesh):
    tok = P(None, AXES, None)

    return jax.shard_map(
        local,
        mesh=mesh,
        in_specs=(tok, tok, tok, tok, P(), P(None, "expert"), P(None, "expert"), P(None, "expert")),
        out_specs=(tok, tok, P("dp", "expert"), P("dp", "expert"), P("dp", "expert")),
        check_vma=False,
    )
```

```python
import math

import jax
import jax.numpy as jnp
from jax import lax
from jax.experimental import pallas as pl
from jax.experimental.pallas import tpu as pltpu
from jax.sharding import PartitionSpec as P


SPLIT = 2
AXES = ("dp", "expert")
PLAIN = (((1,), (0,)), ((), ()))
CONTRACT = (((1,), (1,)), ((), ()))
ROWS_FIRST = (((0,), (0,)), ((), ()))
VMEM = pl.BlockSpec(memory_space=pltpu.VMEM)
SMEM = pl.BlockSpec(memory_space=pltpu.SMEM)
HBM = pl.BlockSpec(memory_space=pltpu.HBM)


def near_groups(n_dp, n_ep):
    groups = []
    for side in range(n_dp):
        for core in range(SPLIT):
            groups.append(
                [((e % n_dp) ^ side) * n_ep + SPLIT * e + core for e in range(n_ep // SPLIT)]
            )
    return groups


def exchange(x, groups):
    return lax.all_to_all(
        x, AXES, split_axis=0, concat_axis=0, tiled=True, axis_index_groups=groups
    )


def mm(a, b, dims=PLAIN):
    return lax.dot_general(a, b, dims, preferred_element_type=jnp.float32)


def bf(*shape):
    return jax.ShapeDtypeStruct(shape, jnp.bfloat16)


def in_vmem(x):
    return pltpu.with_memory_space_constraint(x, pltpu.VMEM)


def in_hbm(x):
    return pltpu.with_memory_space_constraint(x, pltpu.HBM)


def call(kernel, outs, ins, flops, in_specs, out_specs=None, scratch=()):
    size = sum(math.prod(x.shape) * x.dtype.itemsize for x in tuple(ins) + tuple(outs))
    return pl.pallas_call(
        kernel,
        out_shape=outs,
        in_specs=in_specs,
        out_specs=out_specs or [VMEM] * len(outs),
        scratch_shapes=list(scratch),
        compiler_params=pltpu.CompilerParams(vmem_limit_bytes=28 << 20),
        cost_estimate=pl.CostEstimate(flops=flops, bytes_accessed=size, transcendentals=0),
    )(*ins)


def pack_body(slots, capacity, ids_hbm, prob_hbm, marks_hbm, tok_ref, cot_ref,
              sent_ref, pick_ref, split_ref, ids_ref, prob_ref, marks_ref,
              tok_buf, cot_buf, buf, sems):
    small = [
        pltpu.make_async_copy(a, b, sems.at[4 + i])
        for i, (a, b) in enumerate(
            ((ids_hbm, ids_ref), (prob_hbm, prob_ref), (marks_hbm, marks_ref))
        )
    ]
    for copy in small:
        copy.start()
    micros, topk, per_micro = ids_ref.shape
    experts = marks_ref.shape[1]
    places, rows = pick_ref.shape
    width = tok_ref.shape[1]
    fetch_tok = pltpu.make_async_copy(tok_ref, tok_buf, sems.at[0])
    fetch_cot = pltpu.make_async_copy(cot_ref, cot_buf, sems.at[1])
    fetch_tok.start()
    fetch_cot.start()
    for copy in small:
        copy.wait()
    ids = jnp.concatenate([ids_ref[m] for m in range(micros)], axis=1)
    probs = jnp.concatenate([prob_ref[m] for m in range(micros)], axis=1)
    place = lax.broadcasted_iota(jnp.int32, (places, rows), 0)
    token = lax.broadcasted_iota(jnp.int32, (places, rows), 1)
    expert = place // (micros * slots)
    micro = (place // slots) % micros
    hit = jnp.zeros((places, rows), jnp.float32)
    prob = jnp.zeros((places, rows), jnp.float32)
    for k in range(topk):
        same = ids[k : k + 1, :] == expert
        hit = hit + jnp.where(same, 1.0, 0.0)
        prob = prob + jnp.where(same, probs[k : k + 1, :], 0.0)
    down = lax.broadcasted_iota(jnp.int32, (rows, rows), 0)
    across = lax.broadcasted_iota(jnp.int32, (rows, rows), 1)
    earlier = (down < across) & (across // per_micro == down // per_micro)
    earlier = jnp.where(earlier, 1.0, 0.0).astype(jnp.bfloat16)
    ranked = mm(hit.astype(jnp.bfloat16), earlier)
    label = lax.broadcasted_iota(jnp.int32, (places, experts), 1)
    spot = lax.broadcasted_iota(jnp.int32, (places, experts), 0)
    marks = jnp.zeros((places, experts), jnp.float32)
    for m in range(micros):
        mark = jnp.where(marks_ref[m : m + 1, :] > 0, 1.0, 0.0)
        marks = marks + jnp.where((spot // slots) % micros == m, mark, 0.0)
    marks = jnp.where(label == spot // (micros * slots), marks, 0.0)
    limit = capacity * (1.0 + jnp.sum(marks, axis=1, keepdims=True))
    chosen = (hit > 0.5) & (micro == token // per_micro) & (ranked < limit)
    chosen = chosen & (ranked == (place % slots).astype(jnp.float32))
    picked = jnp.where(chosen, 1.0, 0.0).astype(jnp.bfloat16)
    weight = jnp.where(chosen, prob, 0.0)
    slot_prob = jnp.sum(weight, axis=1, keepdims=True)
    high = weight.astype(jnp.bfloat16)
    rest = weight - high.astype(jnp.float32)
    middle = rest.astype(jnp.bfloat16)
    low = (rest - middle.astype(jnp.float32)).astype(jnp.bfloat16)
    pick_ref[...] = picked
    split_ref[:, 0:rows] = high
    split_ref[:, rows : 2 * rows] = middle
    split_ref[:, 2 * rows : 3 * rows] = low
    fetch_tok.wait()
    buf[:, :width] = mm(picked, tok_buf[...]).astype(jnp.bfloat16)
    first = pltpu.make_async_copy(
        buf.at[:, pl.ds(0, width)], sent_ref.at[:, pl.ds(0, width)], sems.at[2]
    )
    first.start()
    fetch_cot.wait()
    buf[:, width:] = (slot_prob * mm(picked, cot_buf[...])).astype(jnp.bfloat16)
    second = pltpu.make_async_copy(
        buf.at[:, pl.ds(width, width)], sent_ref.at[:, pl.ds(width, width)], sems.at[3]
    )
    second.start()
    first.wait()
    second.wait()


def cut_body(start_ref, rows_ref, out_ref, sems):
    take = out_ref.shape[1] // 2
    width = rows_ref.shape[1] // 2
    start = pl.multiple_of(start_ref[0], 128)
    copies = [
        pltpu.make_async_copy(
            rows_ref.at[:, pl.ds(pl.multiple_of(start + i * width, 128), take)],
            out_ref.at[:, pl.ds(i * take, take)],
            sems.at[i],
        )
        for i in range(2)
    ]
    for copy in copies:
        copy.start()
    for copy in copies:
        copy.wait()


def slopes(gate_pre, up_pre, hidden_grad):
    squash = jax.nn.sigmoid(gate_pre)
    active = gate_pre * squash
    hidden = (active * up_pre).astype(jnp.bfloat16)
    slope = squash * (1.0 + gate_pre * (1.0 - squash))
    gate_grad = (hidden_grad * up_pre * slope).astype(jnp.bfloat16)
    up_grad = (hidden_grad * active).astype(jnp.bfloat16)
    return hidden, gate_grad, up_grad


def own_body(pieces, rows_ref, wg_ref, wu_ref, wd_ref, hid_ref, gg_ref, ug_ref,
             wg_out, wu_out, wd_out, xbuf, cbuf, sems):
    width = wg_ref.shape[0]
    size = width // pieces
    fetches = []
    for i in range(pieces):
        low = i * size
        span = pl.ds(low, size)
        moves = (
            (rows_ref.at[:, span], xbuf.at[:, span]),
            (wg_ref.at[span, :], wg_out.at[span, :]),
            (wu_ref.at[span, :], wu_out.at[span, :]),
            (rows_ref.at[:, pl.ds(width + low, size)], cbuf.at[:, span]),
            (wd_ref.at[span, :], wd_out.at[span, :]),
        )
        fetches.append(
            [pltpu.make_async_copy(a, b, sems.at[i, k]) for k, (a, b) in enumerate(moves)]
        )
    for fetch in fetches:
        for copy in fetch:
            copy.start()
    gate_pre = up_pre = hidden_grad = 0.0
    for i in range(pieces):
        low, high = i * size, (i + 1) * size
        for copy in fetches[i]:
            copy.wait()
        x = xbuf[:, low:high]
        gate_pre = gate_pre + mm(x, wg_out[low:high, :])
        up_pre = up_pre + mm(x, wu_out[low:high, :])
        hidden_grad = hidden_grad + mm(cbuf[:, low:high], wd_out[low:high, :])
    values = slopes(gate_pre, up_pre, hidden_grad)
    for ref, value in zip((hid_ref, gg_ref, ug_ref), values):
        ref[...] = value


def oth_body(rows_ref, wg_ref, wu_ref, wd_ref, h_ref, g_ref, u_ref,
             hid_ref, gg_ref, ug_ref):
    width = wg_ref.shape[0]
    x = rows_ref[:, 0:width]
    gate_pre = mm(x, wg_ref[...])
    up_pre = mm(x, wu_ref[...])
    hidden_grad = mm(rows_ref[:, width : 2 * width], wd_ref[...])
    values = slopes(gate_pre, up_pre, hidden_grad)
    rows = h_ref.shape[0]
    for ref, prior, value in zip((hid_ref, gg_ref, ug_ref), (h_ref, g_ref, u_ref), values):
        ref[0:rows, :] = prior[...]
        ref[rows : 2 * rows, :] = value


def out_body(hid_ref, wd_ref, out_ref):
    rows = out_ref.shape[0]
    hidden = hid_ref[rows : 2 * rows, :]
    out_ref[...] = mm(hidden, wd_ref[...], CONTRACT).astype(jnp.bfloat16)


def dx_body(gg_ref, ug_ref, wg_ref, wu_ref, dx_ref):
    rows = dx_ref.shape[0]
    dx = mm(gg_ref[rows : 2 * rows, :], wg_ref[...], CONTRACT)
    dx = dx + mm(ug_ref[rows : 2 * rows, :], wu_ref[...], CONTRACT)
    dx_ref[...] = dx.astype(jnp.bfloat16)


def own_end_body(hid_ref, gg_ref, ug_ref, wg_ref, wu_ref, wd_ref, out_ref):
    rows, double = out_ref.shape
    width = double // 2
    out = mm(hid_ref[0:rows, :], wd_ref[...], CONTRACT)
    out_ref[:, 0:width] = out.astype(jnp.bfloat16)
    dx = mm(gg_ref[0:rows, :], wg_ref[...], CONTRACT)
    dx = dx + mm(ug_ref[0:rows, :], wu_ref[...], CONTRACT)
    out_ref[:, width:double] = dx.astype(jnp.bfloat16)


def add_body(pieces, part_ref, out_ref, dx_ref, total_ref, buf, sems):
    width = out_ref.shape[1]
    size = width // pieces
    copies = []
    for i in range(2 * pieces):
        low = i * size
        source = out_ref if i < pieces else dx_ref
        there = source[:, low % width : low % width + size].astype(jnp.float32)
        here = part_ref[:, low : low + size].astype(jnp.float32)
        buf[:, low : low + size] = (here + there).astype(jnp.bfloat16)
        span = pl.ds(low, size)
        copies.append(pltpu.make_async_copy(buf.at[:, span], total_ref.at[:, span], sems.at[i]))
        copies[i].start()
    for copy in copies:
        copy.wait()


def turn_body(half_ref, first_ref, second_ref, out_ref):
    rows = first_ref.shape[0]
    out_ref[:, 0:rows] = first_ref[...].T
    out_ref[:, rows : 2 * rows] = second_ref[...].T


def turn(half, first, second, cut):
    rows, wide = first.shape
    block = 256
    tall = wide if cut else wide // 2
    steps = tall // block
    per = steps // 2
    if cut:
        spec = pl.BlockSpec((rows, block), lambda i, h: (0, i))
    else:
        spec = pl.BlockSpec((rows, block), lambda i, h: (0, h[0] * per + i + i // per * per))
    return pl.pallas_call(
        turn_body,
        out_shape=bf(tall, 2 * rows),
        grid_spec=pltpu.PrefetchScalarGridSpec(
            num_scalar_prefetch=1,
            grid=(steps,),
            in_specs=[spec, spec],
            out_specs=pl.BlockSpec((block, 2 * rows), lambda i, h: (i, 0)),
        ),
        compiler_params=pltpu.CompilerParams(vmem_limit_bytes=28 << 20),
    )(half, first, second)


def grad_body(near_ref, far_ref, here_ref, there_ref, out_ref):
    out_ref[...] = mm(near_ref[...], here_ref[...]) + mm(far_ref[...], there_ref[...])


def weight_grad(near, far, here, there, second):
    wide, rows = near.shape
    part = here.shape[1]
    tall = wide // 2
    block = 896
    steps = tall // block
    start = steps if second else 0
    lhs = pl.BlockSpec((block, rows), lambda i: (start + i, 0))
    whole = pl.BlockSpec((rows, part), lambda i: (0, 0))
    return pl.pallas_call(
        grad_body,
        out_shape=jax.ShapeDtypeStruct((tall, part), jnp.float32),
        grid=(steps,),
        in_specs=[lhs, lhs, whole, whole],
        out_specs=pl.BlockSpec((block, part), lambda i: (i, 0)),
        compiler_params=pltpu.CompilerParams(vmem_limit_bytes=28 << 20),
        cost_estimate=pl.CostEstimate(
            flops=4 * rows * tall * part, bytes_accessed=8 << 20, transcendentals=0
        ),
    )(near, far, here, there)


def combine_body(pieces, back_ref, pick_ref, split_ref, moe_ref, dx_ref, buf, sems):
    count, width = moe_ref.shape
    size = width // pieces
    copies = []
    for i in range(2 * pieces):
        span = pl.ds(i * size, size)
        copies.append(pltpu.make_async_copy(back_ref.at[:, span], buf.at[:, span], sems.at[i]))
    for copy in copies:
        copy.start()
    for i in range(pieces):
        low, high = i * size, (i + 1) * size
        copies[i].wait()
        sums = mm(split_ref[...], buf[:, low:high], ROWS_FIRST)
        moe = sums[0:count] + (sums[count : 2 * count] + sums[2 * count : 3 * count])
        moe_ref[:, low:high] = moe.astype(jnp.bfloat16)
    for i in range(pieces):
        low, high = i * size, (i + 1) * size
        copies[pieces + i].wait()
        dx = mm(pick_ref[...], buf[:, width + low : width + high], ROWS_FIRST)
        dx_ref[:, low:high] = dx.astype(jnp.bfloat16)


def combine(back, picked, split, pieces):
    places, double = back.shape
    width = double // 2
    rows = picked.shape[1]

    def body(*refs):
        combine_body(pieces, *refs)

    return call(
        body,
        (bf(rows, width), bf(rows, width)),
        (in_hbm(back), picked, split),
        8 * rows * places * width,
        [HBM, VMEM, VMEM],
        scratch=(
            pltpu.VMEM((places, double), jnp.bfloat16),
            pltpu.SemaphoreType.DMA((2 * pieces,)),
        ),
    )


def local(tokens, out_grad, expert_ids, route_probs, copy_marks, w_gate, w_up, w_down):
    n_dp = lax.axis_size("dp")
    n_ep = lax.axis_size("expert")
    devices = n_dp * n_ep
    experts = n_ep // SPLIT
    micros, tok_rows, width = tokens.shape
    topk = expert_ids.shape[2]
    capacity = max(1, tok_rows * topk // experts)
    slots = 2 * capacity
    group_rows = micros * slots
    places = experts * group_rows
    half_width = width // n_dp
    part = w_gate.shape[1]
    flat_rows = micros * tok_rows
    half = lax.axis_index("dp").astype(jnp.int32)
    groups = near_groups(n_dp, n_ep)
    cores = [(i, i ^ 1) for i in range(devices)]
    pairs = [(i, (i + n_ep) % devices) for i in range(devices)]
    unit = 2 * places * part * width

    def core_swap(x):
        return lax.ppermute(x, AXES, cores)

    def pair_swap(x):
        return lax.ppermute(x, AXES, pairs)

    def travel(x):
        return exchange(x.reshape(experts, group_rows, 2 * width), groups).reshape(-1, 2 * width)

    def pack(*refs):
        pack_body(slots, capacity, *refs)

    sent, picked, split = call(
        pack,
        (
            pltpu.HBM((places, 2 * width), jnp.bfloat16),
            bf(places, flat_rows),
            bf(places, 3 * flat_rows),
        ),
        (
            in_hbm(expert_ids.transpose(0, 2, 1)),
            in_hbm(route_probs.transpose(0, 2, 1)),
            in_hbm(copy_marks),
            in_hbm(tokens.reshape(flat_rows, width)),
            in_hbm(out_grad.reshape(flat_rows, width)),
        ),
        4 * places * flat_rows * width,
        [HBM] * 5,
        [HBM, VMEM, VMEM],
        (
            pltpu.VMEM((micros, topk, tok_rows), jnp.int32),
            pltpu.VMEM((micros, topk, tok_rows), jnp.float32),
            pltpu.VMEM((micros, experts), jnp.int32),
            pltpu.VMEM((flat_rows, width), jnp.bfloat16),
            pltpu.VMEM((flat_rows, width), jnp.bfloat16),
            pltpu.VMEM((places, 2 * width), jnp.bfloat16),
            pltpu.SemaphoreType.DMA((7,)),
        ),
    )
    start = ((1 - half) * half_width).reshape(1)
    sent, start = lax.optimization_barrier((sent, start))
    own = travel(sent)
    oth = in_vmem(core_swap(own))
    (theirs,) = call(
        cut_body,
        (bf(places, width),),
        (start, in_hbm(own)),
        0,
        [SMEM, HBM],
        [VMEM],
        (pltpu.SemaphoreType.DMA((2,)),),
    )
    pair_own = pair_swap(theirs)

    pieces = 4

    def begin(*refs):
        own_body(pieces, *refs)

    def finish(*refs):
        add_body(pieces, *refs)

    mid = bf(places, part)
    mids = bf(2 * places, part)
    *first, wg, wu, wd = call(
        begin,
        (mid,) * 3 + (bf(width, part),) * 3,
        tuple(map(in_hbm, (own, w_gate, w_up, w_down))),
        3 * unit,
        [HBM] * 4,
        scratch=(
            pltpu.VMEM((places, width), jnp.bfloat16),
            pltpu.VMEM((places, width), jnp.bfloat16),
            pltpu.SemaphoreType.DMA((pieces, 5)),
        ),
    )
    hid, gg, ug = call(
        oth_body,
        (mids,) * 3,
        (oth, wg, wu, wd, *first),
        3 * unit,
        [VMEM] * 7,
    )
    row = bf(places, width)
    (out_oth,) = call(out_body, (row,), (hid, wd), unit, [VMEM] * 2)
    (dx_oth,) = call(dx_body, (row,), (gg, ug, wg, wu), 2 * unit, [VMEM] * 4)
    out_other = core_swap(out_oth)
    dx_other = core_swap(dx_oth)
    hid_there = pair_swap(hid)
    gg_there = pair_swap(gg)
    ug_there = pair_swap(ug)

    (mine,) = call(
        own_end_body, (bf(places, 2 * width),), (hid, gg, ug, wg, wu, wd), 3 * unit, [VMEM] * 6
    )
    (total,) = call(
        finish,
        (pltpu.HBM((places, 2 * width), jnp.bfloat16),),
        (mine, out_other, dx_other),
        0,
        [VMEM] * 3,
        [HBM],
        (
            pltpu.VMEM((places, 2 * width), jnp.bfloat16),
            pltpu.SemaphoreType.DMA((2 * pieces,)),
        ),
    )
    back = travel(total)
    pair_oth = core_swap(pair_own)
    h = half.reshape(1)
    near = turn(h, own, oth, False)
    far = turn(h, pair_own, pair_oth, True)
    grad_down = weight_grad(near, far, hid, hid_there, True)
    grad_gate = weight_grad(near, far, gg, gg_there, False)
    grad_up = weight_grad(near, far, ug, ug_there, False)
    moe, grad_in = combine(back, picked, split, pieces)
    return (
        moe.reshape(micros, tok_rows, width),
        grad_in.reshape(micros, tok_rows, width),
        grad_gate,
        grad_up,
        grad_down,
    )


def solution(mesh):
    tok = P(None, AXES, None)

    return jax.shard_map(
        local,
        mesh=mesh,
        in_specs=(tok, tok, tok, tok, P(), P(None, "expert"), P(None, "expert"), P(None, "expert")),
        out_specs=(tok, tok, P("dp", "expert"), P("dp", "expert"), P("dp", "expert")),
        check_vma=False,
    )
```

```python
import math

import jax
import jax.numpy as jnp
from jax import lax
from jax.experimental import pallas as pl
from jax.experimental.pallas import tpu as pltpu
from jax.sharding import PartitionSpec as P


SPLIT = 2
AXES = ("dp", "expert")
PLAIN = (((1,), (0,)), ((), ()))
CONTRACT = (((1,), (1,)), ((), ()))
VMEM = pl.BlockSpec(memory_space=pltpu.VMEM)
SMEM = pl.BlockSpec(memory_space=pltpu.SMEM)
HBM = pl.BlockSpec(memory_space=pltpu.HBM)


def near_groups(n_dp, n_ep):
    groups = []
    for side in range(n_dp):
        for core in range(SPLIT):
            groups.append(
                [((e % n_dp) ^ side) * n_ep + SPLIT * e + core for e in range(n_ep // SPLIT)]
            )
    return groups


def exchange(x, groups):
    return lax.all_to_all(
        x, AXES, split_axis=0, concat_axis=0, tiled=True, axis_index_groups=groups
    )


def mm(a, b, dims=PLAIN):
    return lax.dot_general(a, b, dims, preferred_element_type=jnp.float32)


def bf(*shape):
    return jax.ShapeDtypeStruct(shape, jnp.bfloat16)


def in_vmem(x):
    return pltpu.with_memory_space_constraint(x, pltpu.VMEM)


def in_hbm(x):
    return pltpu.with_memory_space_constraint(x, pltpu.HBM)


def call(kernel, outs, ins, flops, in_specs, out_specs=None, scratch=(), aliases=None):
    size = sum(math.prod(x.shape) * x.dtype.itemsize for x in tuple(ins) + tuple(outs))
    return pl.pallas_call(
        kernel,
        out_shape=outs,
        in_specs=in_specs,
        out_specs=out_specs or [VMEM] * len(outs),
        scratch_shapes=list(scratch),
        input_output_aliases=aliases or {},
        compiler_params=pltpu.CompilerParams(vmem_limit_bytes=28 << 20),
        cost_estimate=pl.CostEstimate(flops=flops, bytes_accessed=size, transcendentals=0),
    )(*ins)


def pack_body(slots, capacity, ids_hbm, prob_hbm, marks_hbm, tok_ref, cot_ref, wg_ref,
              sent_ref, pick_ref, split_ref, wg_out, ids_ref, prob_ref, marks_ref,
              tok_buf, cot_buf, buf, sems):
    small = [
        pltpu.make_async_copy(a, b, sems.at[4 + i])
        for i, (a, b) in enumerate(
            ((ids_hbm, ids_ref), (prob_hbm, prob_ref), (marks_hbm, marks_ref))
        )
    ]
    for copy in small:
        copy.start()
    micros, topk, per_micro = ids_ref.shape
    experts = marks_ref.shape[1]
    places, rows = pick_ref.shape
    width = tok_ref.shape[1]
    fetch_tok = pltpu.make_async_copy(tok_ref, tok_buf, sems.at[0])
    fetch_cot = pltpu.make_async_copy(cot_ref, cot_buf, sems.at[1])
    fetch_tok.start()
    fetch_cot.start()
    weight = pltpu.make_async_copy(wg_ref, wg_out, sems.at[7])
    weight.start()
    for copy in small:
        copy.wait()
    ids = jnp.concatenate([ids_ref[m] for m in range(micros)], axis=1)
    probs = jnp.concatenate([prob_ref[m] for m in range(micros)], axis=1)
    place = lax.broadcasted_iota(jnp.int32, (places, rows), 0)
    token = lax.broadcasted_iota(jnp.int32, (places, rows), 1)
    expert = place // (micros * slots)
    micro = (place // slots) % micros
    hit = jnp.zeros((places, rows), jnp.float32)
    prob = jnp.zeros((places, rows), jnp.float32)
    for k in range(topk):
        same = ids[k : k + 1, :] == expert
        hit = hit + jnp.where(same, 1.0, 0.0)
        prob = prob + jnp.where(same, probs[k : k + 1, :], 0.0)
    down = lax.broadcasted_iota(jnp.int32, (rows, rows), 0)
    across = lax.broadcasted_iota(jnp.int32, (rows, rows), 1)
    earlier = (down < across) & (across // per_micro == down // per_micro)
    earlier = jnp.where(earlier, 1.0, 0.0).astype(jnp.bfloat16)
    ranked = mm(hit.astype(jnp.bfloat16), earlier)
    label = lax.broadcasted_iota(jnp.int32, (places, experts), 1)
    spot = lax.broadcasted_iota(jnp.int32, (places, experts), 0)
    marks = jnp.zeros((places, experts), jnp.float32)
    for m in range(micros):
        mark = jnp.where(marks_ref[m : m + 1, :] > 0, 1.0, 0.0)
        marks = marks + jnp.where((spot // slots) % micros == m, mark, 0.0)
    marks = jnp.where(label == spot // (micros * slots), marks, 0.0)
    limit = capacity * (1.0 + jnp.sum(marks, axis=1, keepdims=True))
    chosen = (hit > 0.5) & (micro == token // per_micro) & (ranked < limit)
    chosen = chosen & (ranked == (place % slots).astype(jnp.float32))
    picked = jnp.where(chosen, 1.0, 0.0).astype(jnp.bfloat16)
    mixing = jnp.where(chosen, prob, 0.0)
    slot_prob = jnp.sum(mixing, axis=1, keepdims=True)
    high = mixing.astype(jnp.bfloat16)
    rest = mixing - high.astype(jnp.float32)
    middle = rest.astype(jnp.bfloat16)
    low = (rest - middle.astype(jnp.float32)).astype(jnp.bfloat16)
    pick_ref[...] = picked
    split_ref[:, 0:rows] = high
    split_ref[:, rows : 2 * rows] = middle
    split_ref[:, 2 * rows : 3 * rows] = low
    fetch_tok.wait()
    buf[:, :width] = mm(picked, tok_buf[...]).astype(jnp.bfloat16)
    first = pltpu.make_async_copy(
        buf.at[:, pl.ds(0, width)], sent_ref.at[:, pl.ds(0, width)], sems.at[2]
    )
    first.start()
    fetch_cot.wait()
    buf[:, width:] = (slot_prob * mm(picked, cot_buf[...])).astype(jnp.bfloat16)
    second = pltpu.make_async_copy(
        buf.at[:, pl.ds(width, width)], sent_ref.at[:, pl.ds(width, width)], sems.at[3]
    )
    second.start()
    first.wait()
    second.wait()
    weight.wait()


def cut_body(start_ref, rows_ref, out_ref, sems):
    take = out_ref.shape[1] // 2
    width = rows_ref.shape[1] // 2
    start = pl.multiple_of(start_ref[0], 128)
    copies = [
        pltpu.make_async_copy(
            rows_ref.at[:, pl.ds(pl.multiple_of(start + i * width, 128), take)],
            out_ref.at[:, pl.ds(i * take, take)],
            sems.at[i],
        )
        for i in range(2)
    ]
    for copy in copies:
        copy.start()
    for copy in copies:
        copy.wait()


def slopes(gate_pre, up_pre, hidden_grad):
    squash = jax.nn.sigmoid(gate_pre)
    active = gate_pre * squash
    hidden = (active * up_pre).astype(jnp.bfloat16)
    slope = squash * (1.0 + gate_pre * (1.0 - squash))
    gate_grad = (hidden_grad * up_pre * slope).astype(jnp.bfloat16)
    up_grad = (hidden_grad * active).astype(jnp.bfloat16)
    return hidden, gate_grad, up_grad


def own_body(pieces, rows_ref, wg_ref, wu_ref, wd_ref, hid_ref, gg_ref, ug_ref, wu_out, wd_out,
             sems):
    width = wg_ref.shape[0]
    size = width // pieces
    fetches = [
        [
            pltpu.make_async_copy(
                w.at[pl.ds(i * size, size), :], out.at[pl.ds(i * size, size), :], sems.at[i, k]
            )
            for i in range(pieces)
        ]
        for k, (w, out) in enumerate(((wu_ref, wu_out), (wd_ref, wd_out)))
    ]
    for fetch in fetches:
        for copy in fetch:
            copy.start()
    gate_pre = mm(rows_ref[:, 0:width], wg_ref[...])
    results = []
    for k, out in enumerate((wu_out, wd_out)):
        total = 0.0
        for i in range(pieces):
            low, high = i * size, (i + 1) * size
            fetches[k][i].wait()
            total = total + mm(rows_ref[:, k * width + low : k * width + high], out[low:high, :])
        results.append(total)
    values = slopes(gate_pre, *results)
    for ref, value in zip((hid_ref, gg_ref, ug_ref), values):
        ref[...] = value


def oth_body(rows_ref, wg_ref, wu_ref, wd_ref, h_ref, g_ref, u_ref,
             hid_ref, gg_ref, ug_ref):
    width = wg_ref.shape[0]
    x = rows_ref[:, 0:width]
    gate_pre = mm(x, wg_ref[...])
    up_pre = mm(x, wu_ref[...])
    hidden_grad = mm(rows_ref[:, width : 2 * width], wd_ref[...])
    values = slopes(gate_pre, up_pre, hidden_grad)
    rows = h_ref.shape[0]
    for ref, prior, value in zip((hid_ref, gg_ref, ug_ref), (h_ref, g_ref, u_ref), values):
        ref[0:rows, :] = prior[...]
        ref[rows : 2 * rows, :] = value


def out_body(hid_ref, wd_ref, out_ref):
    rows = out_ref.shape[0]
    hidden = hid_ref[rows : 2 * rows, :]
    out_ref[...] = mm(hidden, wd_ref[...], CONTRACT).astype(jnp.bfloat16)


def dx_body(gg_ref, ug_ref, wg_ref, wu_ref, dx_ref):
    rows = dx_ref.shape[0]
    dx = mm(gg_ref[rows : 2 * rows, :], wg_ref[...], CONTRACT)
    dx = dx + mm(ug_ref[rows : 2 * rows, :], wu_ref[...], CONTRACT)
    dx_ref[...] = dx.astype(jnp.bfloat16)


def own_dx_body(gg_ref, ug_ref, wg_ref, wu_ref, dx_ref):
    rows = dx_ref.shape[0]
    dx = mm(gg_ref[0:rows, :], wg_ref[...], CONTRACT)
    dx = dx + mm(ug_ref[0:rows, :], wu_ref[...], CONTRACT)
    dx_ref[...] = dx.astype(jnp.bfloat16)


def store_sums(pieces, part_of, other_ref, total_ref, start, buf, sems):
    size = other_ref.shape[1] // pieces
    copies = []
    for i in range(pieces):
        low, high = i * size, (i + 1) * size
        here = part_of(low, high).astype(jnp.bfloat16).astype(jnp.float32)
        there = other_ref[:, low:high].astype(jnp.float32)
        buf[:, low:high] = (here + there).astype(jnp.bfloat16)
        copies.append(
            pltpu.make_async_copy(
                buf.at[:, pl.ds(low, size)], total_ref.at[:, pl.ds(start + low, size)], sems.at[i]
            )
        )
        copies[i].start()
    for copy in copies:
        copy.wait()


def own_out_body(pieces, hid_ref, wd_ref, other_ref, total_ref, buf, sems):
    hidden = hid_ref[0 : other_ref.shape[0], :]

    def part_of(low, high):
        return mm(hidden, wd_ref[low:high, :], CONTRACT)

    store_sums(pieces, part_of, other_ref, total_ref, 0, buf, sems)


def add_body(pieces, half_ref, dx_ref, other_ref, total_ref, buf, sems):
    def part_of(low, high):
        return dx_ref[:, low:high]

    store_sums(pieces, part_of, other_ref, total_ref, other_ref.shape[1], buf, sems)


def turn_body(half_ref, first_ref, second_ref, out_ref):
    rows = first_ref.shape[0]
    out_ref[:, 0:rows] = first_ref[...].T
    out_ref[:, rows : 2 * rows] = second_ref[...].T


def turn(half, first, second, cut):
    rows, wide = first.shape
    block = 256
    tall = wide if cut else wide // 2
    steps = tall // block
    per = steps // 2
    if cut:
        spec = pl.BlockSpec((rows, block), lambda i, h: (0, i))
    else:
        spec = pl.BlockSpec((rows, block), lambda i, h: (0, h[0] * per + i + i // per * per))
    return pl.pallas_call(
        turn_body,
        out_shape=bf(tall, 2 * rows),
        grid_spec=pltpu.PrefetchScalarGridSpec(
            num_scalar_prefetch=1,
            grid=(steps,),
            in_specs=[spec, spec],
            out_specs=pl.BlockSpec((block, 2 * rows), lambda i, h: (i, 0)),
        ),
        compiler_params=pltpu.CompilerParams(vmem_limit_bytes=28 << 20),
    )(half, first, second)


def grad_body(near_ref, far_ref, here_ref, there_ref, out_ref):
    out_ref[...] = mm(near_ref[...], here_ref[...]) + mm(far_ref[...], there_ref[...])


def weight_grad(near, far, here, there, second):
    wide, rows = near.shape
    part = here.shape[1]
    tall = wide // 2
    block = 896
    steps = tall // block
    start = steps if second else 0
    lhs = pl.BlockSpec((block, rows), lambda i: (start + i, 0))
    whole = pl.BlockSpec((rows, part), lambda i: (0, 0))
    return pl.pallas_call(
        grad_body,
        out_shape=jax.ShapeDtypeStruct((tall, part), jnp.float32),
        grid=(steps,),
        in_specs=[lhs, lhs, whole, whole],
        out_specs=pl.BlockSpec((block, part), lambda i: (i, 0)),
        compiler_params=pltpu.CompilerParams(vmem_limit_bytes=28 << 20),
        cost_estimate=pl.CostEstimate(
            flops=4 * rows * tall * part, bytes_accessed=8 << 20, transcendentals=0
        ),
    )(near, far, here, there)


def near_body(near_ref, here_ref, sum_ref):
    sum_ref[...] = mm(near_ref[0 : sum_ref.shape[0], :], here_ref[...])


def far_body(pieces, sum_ref, far_ref, there_ref, out_ref, buf, sems):
    size = sum_ref.shape[0] // pieces
    copies = []
    for i in range(pieces):
        low, high = i * size, (i + 1) * size
        buf[low:high, :] = sum_ref[low:high, :] + mm(far_ref[low:high, :], there_ref[...])
        span = pl.ds(low, size)
        copies.append(pltpu.make_async_copy(buf.at[span, :], out_ref.at[span, :], sems.at[i]))
        copies[i].start()
    for copy in copies:
        copy.wait()


def combine_body(pieces, back_ref, pick_ref, split_ref, moe_ref, dx_ref, buf, sems):
    count, width = moe_ref.shape
    size = width // pieces
    copies = []
    for i in range(2 * pieces):
        span = pl.ds(i * size, size)
        copies.append(pltpu.make_async_copy(back_ref.at[:, span], buf.at[:, span], sems.at[i]))
    for copy in copies:
        copy.start()
    split = split_ref[...].T
    picked = pick_ref[...].T
    for i in range(pieces):
        low, high = i * size, (i + 1) * size
        copies[i].wait()
        sums = mm(split, buf[:, low:high])
        moe = sums[0:count] + (sums[count : 2 * count] + sums[2 * count : 3 * count])
        moe_ref[:, low:high] = moe.astype(jnp.bfloat16)
    for i in range(pieces):
        low, high = i * size, (i + 1) * size
        copies[pieces + i].wait()
        dx = mm(picked, buf[:, width + low : width + high])
        dx_ref[:, low:high] = dx.astype(jnp.bfloat16)


def combine(back, picked, split, pieces):
    places, double = back.shape
    width = double // 2
    rows = picked.shape[1]

    def body(*refs):
        combine_body(pieces, *refs)

    return call(
        body,
        (bf(rows, width), bf(rows, width)),
        (in_hbm(back), picked, split),
        8 * rows * places * width,
        [HBM, VMEM, VMEM],
        scratch=(
            pltpu.VMEM((places, double), jnp.bfloat16),
            pltpu.SemaphoreType.DMA((2 * pieces,)),
        ),
    )


def local(tokens, out_grad, expert_ids, route_probs, copy_marks, w_gate, w_up, w_down):
    n_dp = lax.axis_size("dp")
    n_ep = lax.axis_size("expert")
    devices = n_dp * n_ep
    experts = n_ep // SPLIT
    micros, tok_rows, width = tokens.shape
    topk = expert_ids.shape[2]
    capacity = max(1, tok_rows * topk // experts)
    slots = 2 * capacity
    group_rows = micros * slots
    places = experts * group_rows
    half_width = width // n_dp
    part = w_gate.shape[1]
    flat_rows = micros * tok_rows
    half = lax.axis_index("dp").astype(jnp.int32)
    groups = near_groups(n_dp, n_ep)
    cores = [(i, i ^ 1) for i in range(devices)]
    pairs = [(i, (i + n_ep) % devices) for i in range(devices)]
    unit = 2 * places * part * width

    def core_swap(x):
        return lax.ppermute(x, AXES, cores)

    def pair_swap(x):
        return lax.ppermute(x, AXES, pairs)

    def travel(x):
        return exchange(x.reshape(experts, group_rows, 2 * width), groups).reshape(-1, 2 * width)

    def pack(*refs):
        pack_body(slots, capacity, *refs)

    sent, picked, split, wg = call(
        pack,
        (
            pltpu.HBM((places, 2 * width), jnp.bfloat16),
            bf(places, flat_rows),
            bf(places, 3 * flat_rows),
            pltpu.VMEM((width, part), jnp.bfloat16),
        ),
        (
            in_hbm(expert_ids.transpose(0, 2, 1)),
            in_hbm(route_probs.transpose(0, 2, 1)),
            in_hbm(copy_marks),
            in_hbm(tokens.reshape(flat_rows, width)),
            in_hbm(out_grad.reshape(flat_rows, width)),
            in_hbm(w_gate),
        ),
        4 * places * flat_rows * width,
        [HBM] * 6,
        [HBM] + [VMEM] * 3,
        (
            pltpu.VMEM((micros, topk, tok_rows), jnp.int32),
            pltpu.VMEM((micros, topk, tok_rows), jnp.float32),
            pltpu.VMEM((micros, experts), jnp.int32),
            pltpu.VMEM((flat_rows, width), jnp.bfloat16),
            pltpu.VMEM((flat_rows, width), jnp.bfloat16),
            pltpu.VMEM((places, 2 * width), jnp.bfloat16),
            pltpu.SemaphoreType.DMA((8,)),
        ),
    )
    start = ((1 - half) * half_width).reshape(1)
    sent, start = lax.optimization_barrier((sent, start))
    wg = in_vmem(wg)
    own = travel(sent)
    own_near = in_vmem(own)
    oth = in_vmem(core_swap(own_near))
    (theirs,) = call(
        cut_body,
        (bf(places, width),),
        (start, in_hbm(own)),
        0,
        [SMEM, HBM],
        [VMEM],
        (pltpu.SemaphoreType.DMA((2,)),),
    )
    pair_own = pair_swap(theirs)

    pieces = 4

    def begin(*refs):
        own_body(pieces, *refs)

    def finish_out(*refs):
        own_out_body(pieces, *refs)

    def finish_dx(*refs):
        add_body(pieces, *refs)

    mid = bf(places, part)
    mids = bf(2 * places, part)
    *first, wu, wd = call(
        begin,
        (mid,) * 3 + (bf(width, part),) * 2,
        (own_near, wg, in_hbm(w_up), in_hbm(w_down)),
        3 * unit,
        [VMEM, VMEM, HBM, HBM],
        scratch=(pltpu.SemaphoreType.DMA((pieces, 2)),),
    )
    hid, gg, ug = call(
        oth_body,
        (mids,) * 3,
        (oth, wg, wu, wd, *first),
        3 * unit,
        [VMEM] * 7,
    )
    row = bf(places, width)
    (out_oth,) = call(out_body, (row,), (hid, wd), unit, [VMEM] * 2)
    (dx_oth,) = call(dx_body, (row,), (gg, ug, wg, wu), 2 * unit, [VMEM] * 4)
    out_other = core_swap(out_oth)
    dx_other = core_swap(dx_oth)
    hid_there = pair_swap(hid)
    gg_there = pair_swap(gg)
    ug_there = pair_swap(ug)

    room = (
        pltpu.VMEM((places, width), jnp.bfloat16),
        pltpu.SemaphoreType.DMA((pieces,)),
    )
    joined = (pltpu.HBM((places, 2 * width), jnp.bfloat16),)
    (dx_own,) = call(own_dx_body, (row,), (gg, ug, wg, wu), 2 * unit, [VMEM] * 4)
    (total,) = call(
        finish_out, joined, (hid, wd, out_other), unit, [VMEM] * 3, [HBM], room
    )
    (total,) = call(
        finish_dx,
        joined,
        (total, dx_own, dx_other),
        0,
        [HBM, VMEM, VMEM],
        [HBM],
        room,
        aliases={0: 0},
    )
    back = travel(total)
    pair_oth = core_swap(pair_own)
    h = half.reshape(1)
    near = turn(h, own, oth, False)
    far = turn(h, pair_own, pair_oth, True)
    grad_down = weight_grad(near, far, hid, hid_there, True)
    grad_gate = weight_grad(near, far, gg, gg_there, False)
    (up_near,) = call(
        near_body,
        (pltpu.VMEM((half_width, part), jnp.float32),),
        (near, ug),
        2 * unit // n_dp,
        [VMEM] * 2,
    )

    def up_far(*refs):
        far_body(pieces, *refs)

    (grad_up,) = call(
        up_far,
        (pltpu.HBM((half_width, part), jnp.float32),),
        (in_vmem(up_near), far, ug_there),
        2 * unit // n_dp,
        [VMEM] * 3,
        [HBM],
        (
            pltpu.VMEM((half_width, part), jnp.float32),
            pltpu.SemaphoreType.DMA((pieces,)),
        ),
    )
    moe, grad_in = combine(back, picked, split, pieces)
    return (
        moe.reshape(micros, tok_rows, width),
        grad_in.reshape(micros, tok_rows, width),
        grad_gate,
        grad_up,
        grad_down,
    )


def solution(mesh):
    tok = P(None, AXES, None)

    return jax.shard_map(
        local,
        mesh=mesh,
        in_specs=(tok, tok, tok, tok, P(), P(None, "expert"), P(None, "expert"), P(None, "expert")),
        out_specs=(tok, tok, P("dp", "expert"), P("dp", "expert"), P("dp", "expert")),
        check_vma=False,
    )
```

```python
import math

import jax
import jax.numpy as jnp
from jax import lax
from jax.experimental import pallas as pl
from jax.experimental.pallas import tpu as pltpu
from jax.sharding import PartitionSpec as P


SPLIT = 2
AXES = ("dp", "expert")
PLAIN = (((1,), (0,)), ((), ()))
CONTRACT = (((1,), (1,)), ((), ()))
VMEM = pl.BlockSpec(memory_space=pltpu.VMEM)
SMEM = pl.BlockSpec(memory_space=pltpu.SMEM)
HBM = pl.BlockSpec(memory_space=pltpu.HBM)


def near_groups(n_dp, n_ep):
    groups = []
    for side in range(n_dp):
        for core in range(SPLIT):
            groups.append(
                [((e % n_dp) ^ side) * n_ep + SPLIT * e + core for e in range(n_ep // SPLIT)]
            )
    return groups


def exchange(x, groups):
    return lax.all_to_all(
        x, AXES, split_axis=0, concat_axis=0, tiled=True, axis_index_groups=groups
    )


def mm(a, b, dims=PLAIN):
    return lax.dot_general(a, b, dims, preferred_element_type=jnp.float32)


def bf(*shape):
    return jax.ShapeDtypeStruct(shape, jnp.bfloat16)


def in_vmem(x):
    return pltpu.with_memory_space_constraint(x, pltpu.VMEM)


def in_hbm(x):
    return pltpu.with_memory_space_constraint(x, pltpu.HBM)


def call(kernel, outs, ins, flops, in_specs, out_specs=None, scratch=(), aliases=None):
    size = sum(math.prod(x.shape) * x.dtype.itemsize for x in tuple(ins) + tuple(outs))
    return pl.pallas_call(
        kernel,
        out_shape=outs,
        in_specs=in_specs,
        out_specs=out_specs or [VMEM] * len(outs),
        scratch_shapes=list(scratch),
        input_output_aliases=aliases or {},
        compiler_params=pltpu.CompilerParams(vmem_limit_bytes=28 << 20),
        cost_estimate=pl.CostEstimate(flops=flops, bytes_accessed=size, transcendentals=0),
    )(*ins)


def pack_body(slots, capacity, ids_hbm, prob_hbm, marks_hbm, tok_ref, cot_ref, wg_ref,
              sent_ref, pick_ref, split_ref, wg_out, ids_ref, prob_ref, marks_ref,
              tok_buf, cot_buf, buf, sems):
    small = [
        pltpu.make_async_copy(a, b, sems.at[4 + i])
        for i, (a, b) in enumerate(
            ((ids_hbm, ids_ref), (prob_hbm, prob_ref), (marks_hbm, marks_ref))
        )
    ]
    for copy in small:
        copy.start()
    micros, topk, per_micro = ids_ref.shape
    experts = marks_ref.shape[1]
    places, rows = pick_ref.shape
    width = tok_ref.shape[1]
    fetch_tok = pltpu.make_async_copy(tok_ref, tok_buf, sems.at[0])
    fetch_cot = pltpu.make_async_copy(cot_ref, cot_buf, sems.at[1])
    fetch_tok.start()
    fetch_cot.start()
    weight = pltpu.make_async_copy(wg_ref, wg_out, sems.at[7])
    weight.start()
    for copy in small:
        copy.wait()
    ids = jnp.concatenate([ids_ref[m] for m in range(micros)], axis=1)
    probs = jnp.concatenate([prob_ref[m] for m in range(micros)], axis=1)
    place = lax.broadcasted_iota(jnp.int32, (places, rows), 0)
    token = lax.broadcasted_iota(jnp.int32, (places, rows), 1)
    expert = place // (micros * slots)
    micro = (place // slots) % micros
    hit = jnp.zeros((places, rows), jnp.float32)
    prob = jnp.zeros((places, rows), jnp.float32)
    for k in range(topk):
        same = ids[k : k + 1, :] == expert
        hit = hit + jnp.where(same, 1.0, 0.0)
        prob = prob + jnp.where(same, probs[k : k + 1, :], 0.0)
    down = lax.broadcasted_iota(jnp.int32, (rows, rows), 0)
    across = lax.broadcasted_iota(jnp.int32, (rows, rows), 1)
    earlier = (down < across) & (across // per_micro == down // per_micro)
    earlier = jnp.where(earlier, 1.0, 0.0).astype(jnp.bfloat16)
    ranked = mm(hit.astype(jnp.bfloat16), earlier)
    label = lax.broadcasted_iota(jnp.int32, (places, experts), 1)
    spot = lax.broadcasted_iota(jnp.int32, (places, experts), 0)
    marks = jnp.zeros((places, experts), jnp.float32)
    for m in range(micros):
        mark = jnp.where(marks_ref[m : m + 1, :] > 0, 1.0, 0.0)
        marks = marks + jnp.where((spot // slots) % micros == m, mark, 0.0)
    marks = jnp.where(label == spot // (micros * slots), marks, 0.0)
    limit = capacity * (1.0 + jnp.sum(marks, axis=1, keepdims=True))
    chosen = (hit > 0.5) & (micro == token // per_micro) & (ranked < limit)
    chosen = chosen & (ranked == (place % slots).astype(jnp.float32))
    picked = jnp.where(chosen, 1.0, 0.0).astype(jnp.bfloat16)
    mixing = jnp.where(chosen, prob, 0.0)
    slot_prob = jnp.sum(mixing, axis=1, keepdims=True)
    high = mixing.astype(jnp.bfloat16)
    rest = mixing - high.astype(jnp.float32)
    middle = rest.astype(jnp.bfloat16)
    low = (rest - middle.astype(jnp.float32)).astype(jnp.bfloat16)
    pick_ref[...] = picked
    split_ref[:, 0:rows] = high
    split_ref[:, rows : 2 * rows] = middle
    split_ref[:, 2 * rows : 3 * rows] = low
    copies = []
    part = width // 2
    for i in range(4):
        if i == 0:
            fetch_tok.wait()
        if i == 2:
            fetch_cot.wait()
        low = i % 2 * part
        source = tok_buf if i < 2 else cot_buf
        rows_now = mm(picked, source[:, low : low + part])
        if i >= 2:
            rows_now = slot_prob * rows_now
        buf[:, i * part : (i + 1) * part] = rows_now.astype(jnp.bfloat16)
        span = pl.ds(i * part, part)
        copies.append(
            pltpu.make_async_copy(buf.at[:, span], sent_ref.at[:, span], sems.at[8 + i])
        )
        copies[i].start()
    for copy in copies:
        copy.wait()
    weight.wait()


def cut_body(start_ref, rows_ref, out_ref, sems):
    take = out_ref.shape[1] // 2
    width = rows_ref.shape[1] // 2
    start = pl.multiple_of(start_ref[0], 128)
    copies = [
        pltpu.make_async_copy(
            rows_ref.at[:, pl.ds(pl.multiple_of(start + i * width, 128), take)],
            out_ref.at[:, pl.ds(i * take, take)],
            sems.at[i],
        )
        for i in range(2)
    ]
    for copy in copies:
        copy.start()
    for copy in copies:
        copy.wait()


def slopes(gate_pre, up_pre, hidden_grad):
    squash = jax.nn.sigmoid(gate_pre)
    active = gate_pre * squash
    hidden = (active * up_pre).astype(jnp.bfloat16)
    slope = squash * (1.0 + gate_pre * (1.0 - squash))
    gate_grad = (hidden_grad * up_pre * slope).astype(jnp.bfloat16)
    up_grad = (hidden_grad * active).astype(jnp.bfloat16)
    return hidden, gate_grad, up_grad


def own_body(pieces, rows_ref, wg_ref, wu_ref, wd_ref, hid_ref, gg_ref, ug_ref, wu_out, wd_out,
             sems):
    width = wg_ref.shape[0]
    size = width // pieces
    fetches = [
        [
            pltpu.make_async_copy(
                w.at[pl.ds(i * size, size), :], out.at[pl.ds(i * size, size), :], sems.at[i, k]
            )
            for i in range(pieces)
        ]
        for k, (w, out) in enumerate(((wu_ref, wu_out), (wd_ref, wd_out)))
    ]
    for copy in fetches[0]:
        copy.start()
    gate_pre = mm(rows_ref[:, 0:width], wg_ref[...])
    results = []
    for k, out in enumerate((wu_out, wd_out)):
        total = 0.0
        if k == 0:
            fetches[0][0].wait()
            for copy in fetches[1]:
                copy.start()
        for i in range(pieces):
            low, high = i * size, (i + 1) * size
            if k + i > 0:
                fetches[k][i].wait()
            total = total + mm(rows_ref[:, k * width + low : k * width + high], out[low:high, :])
        results.append(total)
    values = slopes(gate_pre, *results)
    for ref, value in zip((hid_ref, gg_ref, ug_ref), values):
        ref[...] = value


def oth_body(rows_ref, wg_ref, wu_ref, wd_ref, h_ref, g_ref, u_ref,
             hid_ref, gg_ref, ug_ref):
    width = wg_ref.shape[0]
    x = rows_ref[:, 0:width]
    gate_pre = mm(x, wg_ref[...])
    up_pre = mm(x, wu_ref[...])
    hidden_grad = mm(rows_ref[:, width : 2 * width], wd_ref[...])
    values = slopes(gate_pre, up_pre, hidden_grad)
    rows = h_ref.shape[0]
    for ref, prior, value in zip((hid_ref, gg_ref, ug_ref), (h_ref, g_ref, u_ref), values):
        ref[0:rows, :] = prior[...]
        ref[rows : 2 * rows, :] = value


def out_body(hid_ref, wd_ref, out_ref):
    rows = out_ref.shape[0]
    hidden = hid_ref[rows : 2 * rows, :]
    out_ref[...] = mm(hidden, wd_ref[...], CONTRACT).astype(jnp.bfloat16)


def dx_body(gg_ref, ug_ref, wg_ref, wu_ref, dx_ref):
    rows = dx_ref.shape[0]
    dx = mm(gg_ref[rows : 2 * rows, :], wg_ref[...], CONTRACT)
    dx = dx + mm(ug_ref[rows : 2 * rows, :], wu_ref[...], CONTRACT)
    dx_ref[...] = dx.astype(jnp.bfloat16)


def own_dx_body(gg_ref, ug_ref, wg_ref, wu_ref, dx_ref):
    rows = dx_ref.shape[0]
    dx = mm(gg_ref[0:rows, :], wg_ref[...], CONTRACT)
    dx = dx + mm(ug_ref[0:rows, :], wu_ref[...], CONTRACT)
    dx_ref[...] = dx.astype(jnp.bfloat16)


def store_sums(pieces, part_of, other_ref, total_ref, start, buf, sems):
    size = other_ref.shape[1] // pieces
    copies = []
    for i in range(pieces):
        low, high = i * size, (i + 1) * size
        here = part_of(low, high).astype(jnp.bfloat16).astype(jnp.float32)
        there = other_ref[:, low:high].astype(jnp.float32)
        buf[:, low:high] = (here + there).astype(jnp.bfloat16)
        copies.append(
            pltpu.make_async_copy(
                buf.at[:, pl.ds(low, size)], total_ref.at[:, pl.ds(start + low, size)], sems.at[i]
            )
        )
        copies[i].start()
    for copy in copies:
        copy.wait()


def own_out_body(pieces, hid_ref, wd_ref, other_ref, total_ref, buf, sems):
    hidden = hid_ref[0 : other_ref.shape[0], :]

    def part_of(low, high):
        return mm(hidden, wd_ref[low:high, :], CONTRACT)

    store_sums(pieces, part_of, other_ref, total_ref, 0, buf, sems)


def add_body(pieces, half_ref, dx_ref, other_ref, total_ref, buf, sems):
    def part_of(low, high):
        return dx_ref[:, low:high]

    store_sums(pieces, part_of, other_ref, total_ref, other_ref.shape[1], buf, sems)


def turn_body(half_ref, first_ref, second_ref, out_ref):
    rows = first_ref.shape[0]
    out_ref[:, 0:rows] = first_ref[...].T
    out_ref[:, rows : 2 * rows] = second_ref[...].T


def turn(half, first, second, cut):
    rows, wide = first.shape
    block = 256
    tall = wide if cut else wide // 2
    steps = tall // block
    per = steps // 2
    if cut:
        spec = pl.BlockSpec((rows, block), lambda i, h: (0, i))
    else:
        spec = pl.BlockSpec((rows, block), lambda i, h: (0, h[0] * per + i + i // per * per))
    return pl.pallas_call(
        turn_body,
        out_shape=bf(tall, 2 * rows),
        grid_spec=pltpu.PrefetchScalarGridSpec(
            num_scalar_prefetch=1,
            grid=(steps,),
            in_specs=[spec, spec],
            out_specs=pl.BlockSpec((block, 2 * rows), lambda i, h: (i, 0)),
        ),
        compiler_params=pltpu.CompilerParams(vmem_limit_bytes=28 << 20),
    )(half, first, second)


def grad_body(near_ref, far_ref, here_ref, there_ref, out_ref):
    out_ref[...] = mm(near_ref[...], here_ref[...]) + mm(far_ref[...], there_ref[...])


def weight_grad(near, far, here, there, second):
    wide, rows = near.shape
    part = here.shape[1]
    tall = wide // 2
    block = 896
    steps = tall // block
    start = steps if second else 0
    lhs = pl.BlockSpec((block, rows), lambda i: (start + i, 0))
    whole = pl.BlockSpec((rows, part), lambda i: (0, 0))
    return pl.pallas_call(
        grad_body,
        out_shape=jax.ShapeDtypeStruct((tall, part), jnp.float32),
        grid=(steps,),
        in_specs=[lhs, lhs, whole, whole],
        out_specs=pl.BlockSpec((block, part), lambda i: (i, 0)),
        compiler_params=pltpu.CompilerParams(vmem_limit_bytes=28 << 20),
        cost_estimate=pl.CostEstimate(
            flops=4 * rows * tall * part, bytes_accessed=8 << 20, transcendentals=0
        ),
    )(near, far, here, there)


def near_body(near_ref, here_ref, sum_ref):
    sum_ref[...] = mm(near_ref[0 : sum_ref.shape[0], :], here_ref[...])


def far_body(pieces, sum_ref, far_ref, there_ref, out_ref, buf, sems):
    size = sum_ref.shape[0] // pieces
    copies = []
    for i in range(pieces):
        low, high = i * size, (i + 1) * size
        buf[low:high, :] = sum_ref[low:high, :] + mm(far_ref[low:high, :], there_ref[...])
        span = pl.ds(low, size)
        copies.append(pltpu.make_async_copy(buf.at[span, :], out_ref.at[span, :], sems.at[i]))
        copies[i].start()
    for copy in copies:
        copy.wait()


def combine_body(pieces, back_ref, pick_ref, split_ref, moe_ref, dx_ref, buf, sems):
    count, width = moe_ref.shape
    size = width // pieces
    copies = []
    for i in range(2 * pieces):
        span = pl.ds(i * size, size)
        copies.append(pltpu.make_async_copy(back_ref.at[:, span], buf.at[:, span], sems.at[i]))
    for copy in copies:
        copy.start()
    split = split_ref[...].T
    picked = pick_ref[...].T
    for i in range(pieces):
        low, high = i * size, (i + 1) * size
        copies[i].wait()
        sums = mm(split, buf[:, low:high])
        moe = sums[0:count] + (sums[count : 2 * count] + sums[2 * count : 3 * count])
        moe_ref[:, low:high] = moe.astype(jnp.bfloat16)
    for i in range(pieces):
        low, high = i * size, (i + 1) * size
        copies[pieces + i].wait()
        dx = mm(picked, buf[:, width + low : width + high])
        dx_ref[:, low:high] = dx.astype(jnp.bfloat16)


def combine(back, picked, split, pieces):
    places, double = back.shape
    width = double // 2
    rows = picked.shape[1]

    def body(*refs):
        combine_body(pieces, *refs)

    return call(
        body,
        (bf(rows, width), bf(rows, width)),
        (in_hbm(back), picked, split),
        8 * rows * places * width,
        [HBM, VMEM, VMEM],
        scratch=(
            pltpu.VMEM((places, double), jnp.bfloat16),
            pltpu.SemaphoreType.DMA((2 * pieces,)),
        ),
    )


def local(tokens, out_grad, expert_ids, route_probs, copy_marks, w_gate, w_up, w_down):
    n_dp = lax.axis_size("dp")
    n_ep = lax.axis_size("expert")
    devices = n_dp * n_ep
    experts = n_ep // SPLIT
    micros, tok_rows, width = tokens.shape
    topk = expert_ids.shape[2]
    capacity = max(1, tok_rows * topk // experts)
    slots = 2 * capacity
    group_rows = micros * slots
    places = experts * group_rows
    half_width = width // n_dp
    part = w_gate.shape[1]
    flat_rows = micros * tok_rows
    half = lax.axis_index("dp").astype(jnp.int32)
    groups = near_groups(n_dp, n_ep)
    cores = [(i, i ^ 1) for i in range(devices)]
    pairs = [(i, (i + n_ep) % devices) for i in range(devices)]
    unit = 2 * places * part * width

    def core_swap(x):
        return lax.ppermute(x, AXES, cores)

    def pair_swap(x):
        return lax.ppermute(x, AXES, pairs)

    def travel(x):
        return exchange(x.reshape(experts, group_rows, 2 * width), groups).reshape(-1, 2 * width)

    def pack(*refs):
        pack_body(slots, capacity, *refs)

    sent, picked, split, wg = call(
        pack,
        (
            pltpu.HBM((places, 2 * width), jnp.bfloat16),
            bf(places, flat_rows),
            bf(places, 3 * flat_rows),
            pltpu.VMEM((width, part), jnp.bfloat16),
        ),
        (
            in_hbm(expert_ids.transpose(0, 2, 1)),
            in_hbm(route_probs.transpose(0, 2, 1)),
            in_hbm(copy_marks),
            in_hbm(tokens.reshape(flat_rows, width)),
            in_hbm(out_grad.reshape(flat_rows, width)),
            in_hbm(w_gate),
        ),
        4 * places * flat_rows * width,
        [HBM] * 6,
        [HBM] + [VMEM] * 3,
        (
            pltpu.VMEM((micros, topk, tok_rows), jnp.int32),
            pltpu.VMEM((micros, topk, tok_rows), jnp.float32),
            pltpu.VMEM((micros, experts), jnp.int32),
            pltpu.VMEM((flat_rows, width), jnp.bfloat16),
            pltpu.VMEM((flat_rows, width), jnp.bfloat16),
            pltpu.VMEM((places, 2 * width), jnp.bfloat16),
            pltpu.SemaphoreType.DMA((12,)),
        ),
    )
    start = ((1 - half) * half_width).reshape(1)
    sent, start = lax.optimization_barrier((sent, start))
    wg = in_vmem(wg)
    own = travel(sent)
    own_near = in_vmem(own)
    oth = in_vmem(core_swap(own_near))
    (theirs,) = call(
        cut_body,
        (bf(places, width),),
        (start, in_hbm(own)),
        0,
        [SMEM, HBM],
        [VMEM],
        (pltpu.SemaphoreType.DMA((2,)),),
    )
    pair_own = pair_swap(theirs)

    pieces = 4

    def begin(*refs):
        own_body(pieces, *refs)

    def finish_out(*refs):
        own_out_body(pieces, *refs)

    def finish_dx(*refs):
        add_body(pieces, *refs)

    mid = bf(places, part)
    mids = bf(2 * places, part)
    *first, wu, wd = call(
        begin,
        (mid,) * 3 + (bf(width, part),) * 2,
        (own_near, wg, in_hbm(w_up), in_hbm(w_down)),
        3 * unit,
        [VMEM, VMEM, HBM, HBM],
        scratch=(pltpu.SemaphoreType.DMA((pieces, 2)),),
    )
    row = bf(places, width)
    hid, gg, ug = call(
        oth_body,
        (mids,) * 3,
        (oth, wg, wu, wd, *first),
        3 * unit,
        [VMEM] * 7,
    )
    (out_oth,) = call(out_body, (row,), (hid, wd), unit, [VMEM] * 2)
    (dx_oth,) = call(dx_body, (row,), (gg, ug, wg, wu), 2 * unit, [VMEM] * 4)
    out_other = core_swap(out_oth)
    dx_other = core_swap(dx_oth)
    hid_there = pair_swap(hid)
    gg_there = pair_swap(gg)
    ug_there = pair_swap(ug)

    room = (
        pltpu.VMEM((places, width), jnp.bfloat16),
        pltpu.SemaphoreType.DMA((pieces,)),
    )
    joined = (pltpu.HBM((places, 2 * width), jnp.bfloat16),)
    (dx_own,) = call(own_dx_body, (row,), (gg, ug, wg, wu), 2 * unit, [VMEM] * 4)
    (total,) = call(
        finish_out, joined, (hid, wd, out_other), unit, [VMEM] * 3, [HBM], room
    )
    (total,) = call(
        finish_dx,
        joined,
        (total, dx_own, dx_other),
        0,
        [HBM, VMEM, VMEM],
        [HBM],
        room,
        aliases={0: 0},
    )
    back = travel(total)
    pair_oth = core_swap(pair_own)
    h = half.reshape(1)
    near = turn(h, own, oth, False)
    far = turn(h, pair_own, pair_oth, True)
    grad_down = weight_grad(near, far, hid, hid_there, True)
    grad_gate = weight_grad(near, far, gg, gg_there, False)
    (up_near,) = call(
        near_body,
        (pltpu.VMEM((half_width, part), jnp.float32),),
        (near, ug),
        2 * unit // n_dp,
        [VMEM] * 2,
    )

    def up_far(*refs):
        far_body(pieces, *refs)

    (grad_up,) = call(
        up_far,
        (pltpu.HBM((half_width, part), jnp.float32),),
        (in_vmem(up_near), far, ug_there),
        2 * unit // n_dp,
        [VMEM] * 3,
        [HBM],
        (
            pltpu.VMEM((half_width, part), jnp.float32),
            pltpu.SemaphoreType.DMA((pieces,)),
        ),
    )
    moe, grad_in = combine(back, picked, split, 2)
    return (
        moe.reshape(micros, tok_rows, width),
        grad_in.reshape(micros, tok_rows, width),
        grad_gate,
        grad_up,
        grad_down,
    )


def solution(mesh):
    tok = P(None, AXES, None)

    return jax.shard_map(
        local,
        mesh=mesh,
        in_specs=(tok, tok, tok, tok, P(), P(None, "expert"), P(None, "expert"), P(None, "expert")),
        out_specs=(tok, tok, P("dp", "expert"), P("dp", "expert"), P("dp", "expert")),
        check_vma=False,
    )
```

```python
import math

import jax
import jax.numpy as jnp
from jax import lax
from jax.experimental import pallas as pl
from jax.experimental.pallas import tpu as pltpu
from jax.sharding import PartitionSpec as P


SPLIT = 2
AXES = ("dp", "expert")
PLAIN = (((1,), (0,)), ((), ()))
CONTRACT = (((1,), (1,)), ((), ()))
VMEM = pl.BlockSpec(memory_space=pltpu.VMEM)
SMEM = pl.BlockSpec(memory_space=pltpu.SMEM)
HBM = pl.BlockSpec(memory_space=pltpu.HBM)


def near_groups(n_dp, n_ep):
    groups = []
    for side in range(n_dp):
        for core in range(SPLIT):
            groups.append(
                [((e % n_dp) ^ side) * n_ep + SPLIT * e + core for e in range(n_ep // SPLIT)]
            )
    return groups


def exchange(x, groups):
    return lax.all_to_all(
        x, AXES, split_axis=0, concat_axis=0, tiled=True, axis_index_groups=groups
    )


def mm(a, b, dims=PLAIN):
    return lax.dot_general(a, b, dims, preferred_element_type=jnp.float32)


def bf(*shape):
    return jax.ShapeDtypeStruct(shape, jnp.bfloat16)


def in_vmem(x):
    return pltpu.with_memory_space_constraint(x, pltpu.VMEM)


def in_hbm(x):
    return pltpu.with_memory_space_constraint(x, pltpu.HBM)


def call(kernel, outs, ins, flops, in_specs, out_specs=None, scratch=(), aliases=None):
    size = sum(math.prod(x.shape) * x.dtype.itemsize for x in tuple(ins) + tuple(outs))
    return pl.pallas_call(
        kernel,
        out_shape=outs,
        in_specs=in_specs,
        out_specs=out_specs or [VMEM] * len(outs),
        scratch_shapes=list(scratch),
        input_output_aliases=aliases or {},
        compiler_params=pltpu.CompilerParams(vmem_limit_bytes=28 << 20),
        cost_estimate=pl.CostEstimate(flops=flops, bytes_accessed=size, transcendentals=0),
    )(*ins)


def pack_body(slots, capacity, ids_hbm, prob_hbm, marks_hbm, tok_ref, cot_ref, wg_ref,
              sent_ref, pick_ref, split_ref, wg_out, ids_ref, prob_ref, marks_ref,
              tok_buf, cot_buf, buf, sems):
    small = [
        pltpu.make_async_copy(a, b, sems.at[4 + i])
        for i, (a, b) in enumerate(
            ((ids_hbm, ids_ref), (prob_hbm, prob_ref), (marks_hbm, marks_ref))
        )
    ]
    for copy in small:
        copy.start()
    micros, topk, per_micro = ids_ref.shape
    experts = marks_ref.shape[1]
    places, rows = pick_ref.shape
    width = tok_ref.shape[1]
    fetch_tok = pltpu.make_async_copy(tok_ref, tok_buf, sems.at[0])
    fetch_cot = pltpu.make_async_copy(cot_ref, cot_buf, sems.at[1])
    fetch_tok.start()
    fetch_cot.start()
    weight = pltpu.make_async_copy(wg_ref, wg_out, sems.at[7])
    weight.start()
    for copy in small:
        copy.wait()
    ids = jnp.concatenate([ids_ref[m] for m in range(micros)], axis=1)
    probs = jnp.concatenate([prob_ref[m] for m in range(micros)], axis=1)
    place = lax.broadcasted_iota(jnp.int32, (places, rows), 0)
    token = lax.broadcasted_iota(jnp.int32, (places, rows), 1)
    expert = place // (micros * slots)
    micro = (place // slots) % micros
    hit = jnp.zeros((places, rows), jnp.float32)
    prob = jnp.zeros((places, rows), jnp.float32)
    for k in range(topk):
        same = ids[k : k + 1, :] == expert
        hit = hit + jnp.where(same, 1.0, 0.0)
        prob = prob + jnp.where(same, probs[k : k + 1, :], 0.0)
    down = lax.broadcasted_iota(jnp.int32, (rows, rows), 0)
    across = lax.broadcasted_iota(jnp.int32, (rows, rows), 1)
    earlier = (down < across) & (across // per_micro == down // per_micro)
    earlier = jnp.where(earlier, 1.0, 0.0).astype(jnp.bfloat16)
    ranked = mm(hit.astype(jnp.bfloat16), earlier)
    label = lax.broadcasted_iota(jnp.int32, (places, experts), 1)
    spot = lax.broadcasted_iota(jnp.int32, (places, experts), 0)
    marks = jnp.zeros((places, experts), jnp.float32)
    for m in range(micros):
        mark = jnp.where(marks_ref[m : m + 1, :] > 0, 1.0, 0.0)
        marks = marks + jnp.where((spot // slots) % micros == m, mark, 0.0)
    marks = jnp.where(label == spot // (micros * slots), marks, 0.0)
    limit = capacity * (1.0 + jnp.sum(marks, axis=1, keepdims=True))
    chosen = (hit > 0.5) & (micro == token // per_micro) & (ranked < limit)
    chosen = chosen & (ranked == (place % slots).astype(jnp.float32))
    picked = jnp.where(chosen, 1.0, 0.0).astype(jnp.bfloat16)
    mixing = jnp.where(chosen, prob, 0.0)
    slot_prob = jnp.sum(mixing, axis=1, keepdims=True)
    high = mixing.astype(jnp.bfloat16)
    rest = mixing - high.astype(jnp.float32)
    middle = rest.astype(jnp.bfloat16)
    low = (rest - middle.astype(jnp.float32)).astype(jnp.bfloat16)
    pick_ref[...] = picked
    split_ref[:, 0:rows] = high
    split_ref[:, rows : 2 * rows] = middle
    split_ref[:, 2 * rows : 3 * rows] = low
    copies = []
    part = width // 2
    for i in range(4):
        if i == 0:
            fetch_tok.wait()
        if i == 2:
            fetch_cot.wait()
        low = i % 2 * part
        source = tok_buf if i < 2 else cot_buf
        rows_now = mm(picked, source[:, low : low + part])
        if i >= 2:
            rows_now = slot_prob * rows_now
        buf[:, i * part : (i + 1) * part] = rows_now.astype(jnp.bfloat16)
        span = pl.ds(i * part, part)
        copies.append(
            pltpu.make_async_copy(buf.at[:, span], sent_ref.at[:, span], sems.at[8 + i])
        )
        copies[i].start()
    for copy in copies:
        copy.wait()
    weight.wait()


def cut_body(start_ref, rows_ref, out_ref, sems):
    take = out_ref.shape[1] // 2
    width = rows_ref.shape[1] // 2
    start = pl.multiple_of(start_ref[0], 128)
    copies = [
        pltpu.make_async_copy(
            rows_ref.at[:, pl.ds(pl.multiple_of(start + i * width, 128), take)],
            out_ref.at[:, pl.ds(i * take, take)],
            sems.at[i],
        )
        for i in range(2)
    ]
    for copy in copies:
        copy.start()
    for copy in copies:
        copy.wait()


def slopes(gate_pre, up_pre, hidden_grad):
    squash = jax.nn.sigmoid(gate_pre)
    active = gate_pre * squash
    hidden = (active * up_pre).astype(jnp.bfloat16)
    slope = squash * (1.0 + gate_pre * (1.0 - squash))
    gate_grad = (hidden_grad * up_pre * slope).astype(jnp.bfloat16)
    up_grad = (hidden_grad * active).astype(jnp.bfloat16)
    return hidden, gate_grad, up_grad


def own_body(pieces, rows_ref, wg_ref, wu_ref, wd_ref, hid_ref, gg_ref, ug_ref, wu_out, wd_out,
             sems):
    width = wg_ref.shape[0]
    size = width // pieces
    fetches = [
        [
            pltpu.make_async_copy(
                w.at[pl.ds(i * size, size), :], out.at[pl.ds(i * size, size), :], sems.at[i, k]
            )
            for i in range(pieces)
        ]
        for k, (w, out) in enumerate(((wu_ref, wu_out), (wd_ref, wd_out)))
    ]
    for copy in fetches[0]:
        copy.start()
    gate_pre = mm(rows_ref[:, 0:width], wg_ref[...])
    results = []
    for k, out in enumerate((wu_out, wd_out)):
        total = 0.0
        if k == 0:
            fetches[0][0].wait()
            for copy in fetches[1]:
                copy.start()
        for i in range(pieces):
            low, high = i * size, (i + 1) * size
            if k + i > 0:
                fetches[k][i].wait()
            total = total + mm(rows_ref[:, k * width + low : k * width + high], out[low:high, :])
        results.append(total)
    values = slopes(gate_pre, *results)
    for ref, value in zip((hid_ref, gg_ref, ug_ref), values):
        ref[...] = value


def oth_body(rows_ref, wg_ref, wu_ref, wd_ref, h_ref, g_ref, u_ref,
             hid_ref, gg_ref, ug_ref):
    width = wg_ref.shape[0]
    x = rows_ref[:, 0:width]
    gate_pre = mm(x, wg_ref[...])
    up_pre = mm(x, wu_ref[...])
    hidden_grad = mm(rows_ref[:, width : 2 * width], wd_ref[...])
    values = slopes(gate_pre, up_pre, hidden_grad)
    rows = h_ref.shape[0]
    for ref, prior, value in zip((hid_ref, gg_ref, ug_ref), (h_ref, g_ref, u_ref), values):
        ref[0:rows, :] = prior[...]
        ref[rows : 2 * rows, :] = value


def out_body(hid_ref, wd_ref, out_ref):
    rows = out_ref.shape[0]
    hidden = hid_ref[rows : 2 * rows, :]
    out_ref[...] = mm(hidden, wd_ref[...], CONTRACT).astype(jnp.bfloat16)


def dx_body(gg_ref, ug_ref, wg_ref, wu_ref, dx_ref):
    rows = dx_ref.shape[0]
    dx = mm(gg_ref[rows : 2 * rows, :], wg_ref[...], CONTRACT)
    dx = dx + mm(ug_ref[rows : 2 * rows, :], wu_ref[...], CONTRACT)
    dx_ref[...] = dx.astype(jnp.bfloat16)


def own_dx_body(gg_ref, ug_ref, wg_ref, wu_ref, dx_ref):
    rows = dx_ref.shape[0]
    dx = mm(gg_ref[0:rows, :], wg_ref[...], CONTRACT)
    dx = dx + mm(ug_ref[0:rows, :], wu_ref[...], CONTRACT)
    dx_ref[...] = dx.astype(jnp.bfloat16)


def store_sums(pieces, part_of, other_ref, total_ref, start, buf, sems):
    size = other_ref.shape[1] // pieces
    copies = []
    for i in range(pieces):
        low, high = i * size, (i + 1) * size
        here = part_of(low, high).astype(jnp.bfloat16).astype(jnp.float32)
        there = other_ref[:, low:high].astype(jnp.float32)
        buf[:, low:high] = (here + there).astype(jnp.bfloat16)
        copies.append(
            pltpu.make_async_copy(
                buf.at[:, pl.ds(low, size)], total_ref.at[:, pl.ds(start + low, size)], sems.at[i]
            )
        )
        copies[i].start()
    for copy in copies:
        copy.wait()


def own_out_body(pieces, hid_ref, wd_ref, other_ref, total_ref, buf, sems):
    hidden = hid_ref[0 : other_ref.shape[0], :]

    def part_of(low, high):
        return mm(hidden, wd_ref[low:high, :], CONTRACT)

    store_sums(pieces, part_of, other_ref, total_ref, 0, buf, sems)


def add_body(pieces, half_ref, dx_ref, other_ref, total_ref, buf, sems):
    def part_of(low, high):
        return dx_ref[:, low:high]

    store_sums(pieces, part_of, other_ref, total_ref, other_ref.shape[1], buf, sems)


def turn_body(half_ref, first_ref, second_ref, out_ref):
    rows = first_ref.shape[0]
    out_ref[:, 0:rows] = first_ref[...].T
    out_ref[:, rows : 2 * rows] = second_ref[...].T


def turn(half, first, second, cut):
    rows, wide = first.shape
    block = 256
    tall = wide if cut else wide // 2
    steps = tall // block
    per = steps // 2
    if cut:
        spec = pl.BlockSpec((rows, block), lambda i, h: (0, i))
    else:
        spec = pl.BlockSpec((rows, block), lambda i, h: (0, h[0] * per + i + i // per * per))
    return pl.pallas_call(
        turn_body,
        out_shape=bf(tall, 2 * rows),
        grid_spec=pltpu.PrefetchScalarGridSpec(
            num_scalar_prefetch=1,
            grid=(steps,),
            in_specs=[spec, spec],
            out_specs=pl.BlockSpec((block, 2 * rows), lambda i, h: (i, 0)),
        ),
        compiler_params=pltpu.CompilerParams(vmem_limit_bytes=28 << 20),
    )(half, first, second)


def grad_body(near_ref, far_ref, here_ref, there_ref, out_ref):
    out_ref[...] = mm(near_ref[...], here_ref[...]) + mm(far_ref[...], there_ref[...])


def weight_grad(near, far, here, there, second):
    wide, rows = near.shape
    part = here.shape[1]
    tall = wide // 2
    block = 896
    steps = tall // block
    start = steps if second else 0
    lhs = pl.BlockSpec((block, rows), lambda i: (start + i, 0))
    whole = pl.BlockSpec((rows, part), lambda i: (0, 0))
    return pl.pallas_call(
        grad_body,
        out_shape=jax.ShapeDtypeStruct((tall, part), jnp.float32),
        grid=(steps,),
        in_specs=[lhs, lhs, whole, whole],
        out_specs=pl.BlockSpec((block, part), lambda i: (i, 0)),
        compiler_params=pltpu.CompilerParams(vmem_limit_bytes=28 << 20),
        cost_estimate=pl.CostEstimate(
            flops=4 * rows * tall * part, bytes_accessed=8 << 20, transcendentals=0
        ),
    )(near, far, here, there)


def near_body(near_ref, here_ref, sum_ref):
    sum_ref[...] = mm(near_ref[0 : sum_ref.shape[0], :], here_ref[...])


def far_body(pieces, sum_ref, far_ref, there_ref, out_ref, buf, sems):
    size = sum_ref.shape[0] // pieces
    copies = []
    for i in range(pieces):
        low, high = i * size, (i + 1) * size
        buf[low:high, :] = sum_ref[low:high, :] + mm(far_ref[low:high, :], there_ref[...])
        span = pl.ds(low, size)
        copies.append(pltpu.make_async_copy(buf.at[span, :], out_ref.at[span, :], sems.at[i]))
        copies[i].start()
    for copy in copies:
        copy.wait()


def combine_body(pieces, back_ref, pick_ref, split_ref, moe_hbm, dx_hbm, buf, moe_ref, dx_ref, sems):
    count, width = moe_ref.shape
    size = width // pieces
    copies = []
    for i in range(2 * pieces):
        span = pl.ds(i * size, size)
        copies.append(pltpu.make_async_copy(back_ref.at[:, span], buf.at[:, span], sems.at[i]))
    for copy in copies:
        copy.start()
    split = split_ref[...].T
    picked = pick_ref[...].T
    for i in range(pieces):
        low, high = i * size, (i + 1) * size
        copies[i].wait()
        sums = mm(split, buf[:, low:high])
        moe = sums[0:count] + (sums[count : 2 * count] + sums[2 * count : 3 * count])
        moe_ref[:, low:high] = moe.astype(jnp.bfloat16)
    stores = [pltpu.make_async_copy(moe_ref, moe_hbm, sems.at[2 * pieces])]
    stores[0].start()
    for i in range(pieces):
        low, high = i * size, (i + 1) * size
        copies[pieces + i].wait()
        dx = mm(picked, buf[:, width + low : width + high])
        dx_ref[:, low:high] = dx.astype(jnp.bfloat16)
        span = pl.ds(low, size)
        stores.append(
            pltpu.make_async_copy(
                dx_ref.at[:, span], dx_hbm.at[:, span], sems.at[2 * pieces + 1 + i]
            )
        )
        stores[i + 1].start()
    for store in stores:
        store.wait()


def combine(back, picked, split, pieces):
    places, double = back.shape
    width = double // 2
    rows = picked.shape[1]

    def body(*refs):
        combine_body(pieces, *refs)

    return call(
        body,
        (pltpu.HBM((rows, width), jnp.bfloat16),) * 2,
        (in_hbm(back), picked, split),
        8 * rows * places * width,
        [HBM, VMEM, VMEM],
        [HBM] * 2,
        scratch=(
            pltpu.VMEM((places, double), jnp.bfloat16),
            pltpu.VMEM((rows, width), jnp.bfloat16),
            pltpu.VMEM((rows, width), jnp.bfloat16),
            pltpu.SemaphoreType.DMA((3 * pieces + 1,)),
        ),
    )


def local(tokens, out_grad, expert_ids, route_probs, copy_marks, w_gate, w_up, w_down):
    n_dp = lax.axis_size("dp")
    n_ep = lax.axis_size("expert")
    devices = n_dp * n_ep
    experts = n_ep // SPLIT
    micros, tok_rows, width = tokens.shape
    topk = expert_ids.shape[2]
    capacity = max(1, tok_rows * topk // experts)
    slots = 2 * capacity
    group_rows = micros * slots
    places = experts * group_rows
    half_width = width // n_dp
    part = w_gate.shape[1]
    flat_rows = micros * tok_rows
    half = lax.axis_index("dp").astype(jnp.int32)
    groups = near_groups(n_dp, n_ep)
    cores = [(i, i ^ 1) for i in range(devices)]
    pairs = [(i, (i + n_ep) % devices) for i in range(devices)]
    unit = 2 * places * part * width

    def core_swap(x):
        return lax.ppermute(x, AXES, cores)

    def pair_swap(x):
        return lax.ppermute(x, AXES, pairs)

    def travel(x):
        return exchange(x.reshape(experts, group_rows, 2 * width), groups).reshape(-1, 2 * width)

    def pack(*refs):
        pack_body(slots, capacity, *refs)

    sent, picked, split, wg = call(
        pack,
        (
            pltpu.HBM((places, 2 * width), jnp.bfloat16),
            bf(places, flat_rows),
            bf(places, 3 * flat_rows),
            pltpu.VMEM((width, part), jnp.bfloat16),
        ),
        (
            in_hbm(expert_ids.transpose(0, 2, 1)),
            in_hbm(route_probs.transpose(0, 2, 1)),
            in_hbm(copy_marks),
            in_hbm(tokens.reshape(flat_rows, width)),
            in_hbm(out_grad.reshape(flat_rows, width)),
            in_hbm(w_gate),
        ),
        4 * places * flat_rows * width,
        [HBM] * 6,
        [HBM] + [VMEM] * 3,
        (
            pltpu.VMEM((micros, topk, tok_rows), jnp.int32),
            pltpu.VMEM((micros, topk, tok_rows), jnp.float32),
            pltpu.VMEM((micros, experts), jnp.int32),
            pltpu.VMEM((flat_rows, width), jnp.bfloat16),
            pltpu.VMEM((flat_rows, width), jnp.bfloat16),
            pltpu.VMEM((places, 2 * width), jnp.bfloat16),
            pltpu.SemaphoreType.DMA((12,)),
        ),
    )
    start = ((1 - half) * half_width).reshape(1)
    sent, start = lax.optimization_barrier((sent, start))
    wg = in_vmem(wg)
    own = travel(sent)
    own_near = in_vmem(own)
    oth = in_vmem(core_swap(own_near))
    (theirs,) = call(
        cut_body,
        (bf(places, width),),
        (start, in_hbm(own)),
        0,
        [SMEM, HBM],
        [VMEM],
        (pltpu.SemaphoreType.DMA((2,)),),
    )
    pair_own = pair_swap(theirs)

    pieces = 4

    def begin(*refs):
        own_body(pieces, *refs)

    def finish_out(*refs):
        own_out_body(pieces, *refs)

    def finish_dx(*refs):
        add_body(pieces, *refs)

    mid = bf(places, part)
    mids = bf(2 * places, part)
    *first, wu, wd = call(
        begin,
        (mid,) * 3 + (bf(width, part),) * 2,
        (own_near, wg, in_hbm(w_up), in_hbm(w_down)),
        3 * unit,
        [VMEM, VMEM, HBM, HBM],
        scratch=(pltpu.SemaphoreType.DMA((pieces, 2)),),
    )
    row = bf(places, width)
    hid, gg, ug = call(
        oth_body,
        (mids,) * 3,
        (oth, wg, wu, wd, *first),
        3 * unit,
        [VMEM] * 7,
    )
    (out_oth,) = call(out_body, (row,), (hid, wd), unit, [VMEM] * 2)
    (dx_oth,) = call(dx_body, (row,), (gg, ug, wg, wu), 2 * unit, [VMEM] * 4)
    out_other = core_swap(out_oth)
    dx_other = core_swap(dx_oth)
    hid_there = pair_swap(hid)
    gg_there = pair_swap(gg)
    ug_there = pair_swap(ug)

    room = (
        pltpu.VMEM((places, width), jnp.bfloat16),
        pltpu.SemaphoreType.DMA((pieces,)),
    )
    joined = (pltpu.HBM((places, 2 * width), jnp.bfloat16),)
    (dx_own,) = call(own_dx_body, (row,), (gg, ug, wg, wu), 2 * unit, [VMEM] * 4)
    (total,) = call(
        finish_out, joined, (hid, wd, out_other), unit, [VMEM] * 3, [HBM], room
    )
    (total,) = call(
        finish_dx,
        joined,
        (total, dx_own, dx_other),
        0,
        [HBM, VMEM, VMEM],
        [HBM],
        room,
        aliases={0: 0},
    )
    back = travel(total)
    pair_oth = core_swap(pair_own)
    h = half.reshape(1)
    near = turn(h, own, oth, False)
    far = turn(h, pair_own, pair_oth, True)
    grad_down = weight_grad(near, far, hid, hid_there, True)
    grad_gate = weight_grad(near, far, gg, gg_there, False)
    (up_near,) = call(
        near_body,
        (pltpu.VMEM((half_width, part), jnp.float32),),
        (near, ug),
        2 * unit // n_dp,
        [VMEM] * 2,
    )

    def up_far(*refs):
        far_body(pieces, *refs)

    (grad_up,) = call(
        up_far,
        (pltpu.HBM((half_width, part), jnp.float32),),
        (in_vmem(up_near), far, ug_there),
        2 * unit // n_dp,
        [VMEM] * 3,
        [HBM],
        (
            pltpu.VMEM((half_width, part), jnp.float32),
            pltpu.SemaphoreType.DMA((pieces,)),
        ),
    )
    moe, grad_in = combine(back, picked, split, 2)
    return (
        moe.reshape(micros, tok_rows, width),
        grad_in.reshape(micros, tok_rows, width),
        grad_gate,
        grad_up,
        grad_down,
    )


def solution(mesh):
    tok = P(None, AXES, None)

    return jax.shard_map(
        local,
        mesh=mesh,
        in_specs=(tok, tok, tok, tok, P(), P(None, "expert"), P(None, "expert"), P(None, "expert")),
        out_specs=(tok, tok, P("dp", "expert"), P("dp", "expert"), P("dp", "expert")),
        check_vma=False,
    )
```
